512 devices in a mesh: row: 16 (over z, core), col: 32 (over y, x).
Axes of the slice: x: 4, y: 8, z: 8, core: 2. Of those that a mesh axis runs over, the one named last changes fastest.
Arguments:
- initial_voltage: float32 [16, 64, 128, 128], P('row', 'col'), may hold values from -6 to 6
- inject: float32 [16, 64, 128, 128], P('row', 'col'), may hold values from -6 to 6
- conduct: float32 [16, 64, 128, 128], P('row', 'col'), as said below
- capacitance: float32 [16, 64, 128], P('row', 'col'), may hold values from 1 to 4
- track_gain: float32 [16, 64, 2, 32], P('row', 'col'), may hold values from 0.3 to 3
- driver_tile: int32 [16, 32, 64], P('row', 'col'), may hold values from 0 to 1
- sink_net: int32 [16, 32, 32, 8], P('row', 'col'), may hold values from 0 to 63
- sink_count: int32 [16, 32, 32], P('row', 'col'), may hold values from 0 to 8, as said below
- sink_tile: int32 [16, 32, 32, 8], P('row', 'col'), may hold values from 0 to 1
- sink_node: int32 [16, 32, 32, 8], P('row', 'col'), may hold values from 0 to 127
- sink_gain: float32 [16, 32, 32, 8], P('row', 'col'), may hold values from 0.5 to 2
Outputs:
- voltage: float32 [16, 64, 128, 128], P('row', 'col')
The draws below stay inside these ranges and needn't reach their ends.
Inputs may be any that keep to these rules, and one draw needn't show every extreme that they name: Slots k >= sink_count[d, s] are ignored; some receiving device takes all 8 slots from some source device in every draw. `conduct`: each tile's block is symmetric with non-positive entries off the diagonal and rows summing to zero.
All inputs are finite; a program needn't handle non-finite values.
Results may differ from the reference program's by a relative error of at most 0.0001.
Values sent between devices are 32-bit elements; how exact they have to be, the bound alone decides.
A program may use at most 64 MiB of HBM per device.

```python
import math
import jax
import jax.numpy as jnp
from jax import lax

NODE = 128
EDGE = 32
PAT = 128
TR = 1
TC = 2
NETS = 64
SLOT = 8
ITERS = 3
STEPS = 1
TILES = 2
GR = 16
GC = 64
N_ROW = 16
N_COL = 32


def draw_conduct(key, part):
    key_base = jax.random.fold_in(key, 0)
    uniform_draw = jax.random.uniform(key_base, (GR, GC, NODE, NODE), jnp.float32)
    weights = 0.6 * uniform_draw ** 16
    weights = 0.5 * (weights + jnp.swapaxes(weights, -1, -2))
    identity = jnp.eye(NODE, dtype=jnp.float32)
    weights = weights * (1.0 - identity)
    degree = jnp.sum(weights, axis=-1)
    return degree[..., :, None] * identity - weights


def draw_sink_count(key, part):
    key_count, key_spot = jax.random.split(key)
    counts = jax.random.randint(key_count, (N_ROW, N_COL, N_COL), 0, SLOT + 1)
    position = jax.random.randint(key_spot, (), 0, N_ROW * N_COL * N_COL)
    flat_counts = counts.reshape(-1).at[position].set(SLOT)
    return flat_counts.reshape((N_ROW, N_COL, N_COL)).astype(jnp.int32)


def plant(entries, key, low, high):
    dims = entries.shape
    index_at = [jax.random.randint(jax.random.fold_in(key, axis), (), 0, dims[axis]) for axis in range(len(dims))]
    entries = entries.at[tuple(index_at)].set(low)
    longest = dims.index(max(dims))
    index_at[longest] = (index_at[longest] + 1) % dims[longest]
    return entries.at[tuple(index_at)].set(high)


def block_levels(rng, dims, cuts, smallest, high):
    level = 1.0
    for dim, shards_of in cuts:
        heights = jax.random.uniform(jax.random.fold_in(jax.random.fold_in(rng, 6), dim), (shards_of,), jnp.float32, smallest / len(cuts), high / len(cuts))
        level = level * jnp.repeat(jnp.exp(heights), dims[dim] // shards_of).reshape((-1,) + (1,) * (len(dims) - 1 - dim))
    return level


def centred(stream_key, shape, scale, limit, cuts=(), kind=jnp.bfloat16):
    factor_of = block_levels(stream_key, shape, cuts, -0.22, 0.18) if cuts else 1.0
    entries = jax.random.normal(stream_key, shape, jnp.float32) * scale * factor_of
    return jnp.minimum(jnp.maximum(entries, -limit), limit).astype(kind)


def setup_inputs(seed: int = 0) -> dict:
    keys = jax.random.split(jax.random.key(seed), 12)
    initial_voltage = centred(keys[0], (GR, GC, NODE, PAT), 1.0, 6.0, ((0, 16), (1, 32)), jnp.float32)
    inject = centred(keys[1], (GR, GC, NODE, PAT), 1.0, 6.0, ((0, 16), (1, 32)), jnp.float32)
    conduct = draw_conduct(jax.random.fold_in(keys[11], 71), 0)
    capacitance = jnp.clip(jnp.exp(math.log(4.0) - 1.3862944 * jax.random.uniform(keys[3], (GR, GC, NODE), jnp.float32) ** block_levels(keys[3], (GR, GC, NODE), ((0, 16), (1, 32)), -0.2, 0.2)), 1.0, 4.0)
    track_gain = jnp.clip(jnp.exp(math.log(3.0) - 2.3025851 * jax.random.uniform(keys[4], (GR, GC, 2, EDGE), jnp.float32) ** block_levels(keys[4], (GR, GC, 2, EDGE), ((0, 16), (1, 32)), -0.2, 0.2)), 0.3, 3.0)
    driver_tile = plant(jax.random.randint(keys[5], (N_ROW, N_COL, NETS), 0, TILES), jax.random.fold_in(keys[5], 1), 0, TILES - 1).astype(jnp.int32)
    sink_net = plant(jax.random.randint(keys[6], (N_ROW, N_COL, N_COL, SLOT), 0, NETS), jax.random.fold_in(keys[6], 1), 0, NETS - 1).astype(jnp.int32)
    sink_count = draw_sink_count(jax.random.fold_in(keys[11], 71), 0)
    sink_tile = plant(jax.random.randint(keys[8], (N_ROW, N_COL, N_COL, SLOT), 0, TILES), jax.random.fold_in(keys[8], 1), 0, TILES - 1).astype(jnp.int32)
    sink_node = plant(jax.random.randint(keys[9], (N_ROW, N_COL, N_COL, SLOT), 0, NODE), jax.random.fold_in(keys[9], 1), 0, NODE - 1).astype(jnp.int32)
    sink_gain = jnp.clip(jnp.exp(math.log(2.0) - 1.3862944 * jax.random.uniform(keys[10], (N_ROW, N_COL, N_COL, SLOT), jnp.float32) ** block_levels(keys[10], (N_ROW, N_COL, N_COL, SLOT), ((0, 16), (1, 32)), -0.2, 0.2)), 0.5, 2.0)
    return dict(initial_voltage=initial_voltage, inject=inject, conduct=conduct, capacitance=capacitance, track_gain=track_gain, driver_tile=driver_tile, sink_net=sink_net, sink_count=sink_count, sink_tile=sink_tile, sink_node=sink_node, sink_gain=sink_gain)


PRECISE = lax.Precision.HIGHEST

def tile_inverse(conduct, capacitance):
    node_count = conduct.shape[-1]
    identity = jnp.eye(node_count, dtype=jnp.float32)
    whole_block = conduct + capacitance[..., None] * identity
    flat_blocks = whole_block.reshape((-1, node_count, node_count))
    factors = jnp.linalg.cholesky(flat_blocks)
    inverse = jax.vmap(lambda factor: jax.scipy.linalg.cho_solve((factor, True), identity))(factors)
    return inverse.reshape(whole_block.shape)

def combine_tracks(inner_part, rim_cells, padded, track_pad):
    edge_count = rim_cells.shape[2]
    east_gain = track_pad[1:-1, 1:-1, 0][..., None]
    west_gain = track_pad[1:-1, :-2, 0][..., None]
    south_gain = track_pad[1:-1, 1:-1, 1][..., None]
    north_gain = track_pad[:-2, 1:-1, 1][..., None]
    track_flow = east_gain * (rim_cells - padded[1:-1, 2:]) + west_gain * (rim_cells - padded[1:-1, :-2])
    track_flow = track_flow + south_gain * (rim_cells - padded[2:, 1:-1]) + north_gain * (rim_cells - padded[:-2, 1:-1])
    return jnp.concatenate([inner_part[:, :, :edge_count] + track_flow, inner_part[:, :, edge_count:]], axis=2)

def apply_grid(voltage, conduct, capacitance, track_pad):
    edge_count = track_pad.shape[-1]
    inner_part = jnp.einsum('rcij,rcjp->rcip', conduct, voltage, precision=PRECISE) + capacitance[..., None] * voltage
    rim_cells = voltage[:, :, :edge_count, :]
    padded = jnp.pad(rim_cells, ((1, 1), (1, 1), (0, 0), (0, 0)))
    return combine_tracks(inner_part, rim_cells, padded, track_pad)

def precondition(inverse, residual):
    return jnp.einsum('rcij,rcjp->rcip', inverse, residual, precision=PRECISE)

def inner_sum(left_vec, right_vec):
    return jnp.sum(left_vec * right_vec, axis=(0, 1, 2))

def by_device(array):
    shaped = array.reshape((N_ROW, TR, N_COL, TC) + array.shape[2:])
    moved = jnp.moveaxis(shaped, 2, 1)
    return moved.reshape((N_ROW, N_COL, TR * TC) + array.shape[2:])

def from_device(array):
    shaped = array.reshape((N_ROW, N_COL, TR, TC) + array.shape[3:])
    moved = jnp.moveaxis(shaped, 1, 2)
    return moved.reshape((N_ROW * TR, N_COL * TC) + array.shape[3:])

def sink_injection(voltage, driver_tile, sink_net, sink_count, sink_tile, sink_node, sink_gain):
    node_count = voltage.shape[2]
    pattern_count = voltage.shape[3]
    device_volts = by_device(voltage).reshape((N_ROW, N_COL, TR * TC * node_count, pattern_count))
    net_count = driver_tile.shape[-1]
    driver_rows = driver_tile * node_count + jnp.arange(net_count, dtype=jnp.int32) % node_count
    driver = jnp.take_along_axis(device_volts, driver_rows[..., None], axis=2)
    row_ids = jnp.arange(N_ROW, dtype=jnp.int32)[:, None, None, None]
    col_ids = jnp.arange(N_COL, dtype=jnp.int32)[None, :, None, None]
    source_ids = jnp.arange(N_COL, dtype=jnp.int32)[None, None, :, None]
    values = driver[row_ids, source_ids, sink_net]
    slot_ids = jnp.arange(sink_net.shape[-1], dtype=jnp.int32)
    weight = jnp.where(slot_ids < sink_count[..., None], sink_gain, jnp.float32(0.0))
    target = sink_tile * node_count + sink_node
    injected = jnp.zeros(device_volts.shape, jnp.float32)
    injected = injected.at[row_ids, col_ids, target].add(values * weight[..., None])
    return from_device(injected.reshape((N_ROW, N_COL, TR * TC, node_count, pattern_count)))

def solve_step(right_side, initial, conduct, capacitance, track_pad, inverse):
    solution = initial
    residual = right_side - apply_grid(initial, conduct, capacitance, track_pad)
    precond = precondition(inverse, residual)
    direction = precond
    rz_now = inner_sum(residual, precond)
    for sweep_idx in range(ITERS):
        applied = apply_grid(direction, conduct, capacitance, track_pad)
        step_size = rz_now / inner_sum(direction, applied)
        solution = solution + step_size * direction
        residual = residual - step_size * applied
        precond = precondition(inverse, residual)
        rz_fresh = inner_sum(residual, precond)
        direction = precond + rz_fresh / rz_now * direction
        rz_now = rz_fresh
    return solution

def reference(initial_voltage, inject, conduct, capacitance, track_gain, driver_tile, sink_net, sink_count, sink_tile, sink_node, sink_gain):
    inverse = tile_inverse(conduct, capacitance)
    track_pad = jnp.pad(track_gain, ((1, 1), (1, 1), (0, 0), (0, 0)))
    voltage = initial_voltage
    for time_step in range(STEPS):
        injected = sink_injection(voltage, driver_tile, sink_net, sink_count, sink_tile, sink_node, sink_gain)
        right_side = capacitance[..., None] * voltage + inject + injected
        voltage = solve_step(right_side, voltage, conduct, capacitance, track_pad, inverse)
    return voltage
```

```python
import functools

import jax
import jax.numpy as jnp
from jax import lax
from jax.experimental import pallas as pl
from jax.experimental.pallas import tpu as pltpu
from jax.sharding import PartitionSpec as P

F32 = jnp.float32
HIGH = lax.Precision.HIGHEST
MESH = pl.DeviceIdType.MESH
SCALE = 1.0 / 32.0
PIVOTS = 4


def dot(left, right):
    return jnp.dot(left, right, precision=HIGH, preferred_element_type=F32)


def lane_splat(block, lane):
    return jnp.take_along_axis(block, jnp.full(block.shape, lane, jnp.int32), axis=1)


def pivot_rows(rows, first, offset, lane):
    mine = [rows[offset + i : offset + i + 1] for i in range(PIVOTS)]
    splats = [lane_splat(rows, first + j) for j in range(PIVOTS)]
    small = [
        [splats[j][offset + i : offset + i + 1] for j in range(PIVOTS)]
        for i in range(PIVOTS)
    ]
    for j in range(PIVOTS):
        scale = 1.0 / small[j][j]
        row = [scale if m == j else small[j][m] * scale for m in range(PIVOTS)]
        for i in range(PIVOTS):
            if i == j:
                continue
            factor = small[i][j]
            small[i] = [
                -factor * scale if m == j else small[i][m] - factor * row[m]
                for m in range(PIVOTS)
            ]
        small[j] = row
    fresh = []
    for i in range(PIVOTS):
        total = small[i][0] * mine[0]
        for j in range(1, PIVOTS):
            total = total + small[i][j] * mine[j]
        for j in range(PIVOTS):
            total = jnp.where(lane == first + j, small[i][j], total)
        fresh.append(total)
    return fresh


def eliminate(mats, start, stop):
    nodes = mats[0].shape[0]
    lane = lax.broadcasted_iota(jnp.int32, (1, nodes), 1)

    def group(index, carry):
        base = pl.multiple_of(index * 8, 8)
        for offset in range(0, 8, PIVOTS):
            first = base + offset
            whole = [mat[...] for mat in mats]
            rows = [mat[pl.ds(base, 8), :] for mat in mats]
            fresh = [pivot_rows(r, first, offset, lane) for r in rows]
            kept = (lane >= first) & (lane < first + PIVOTS)
            done = []
            for t in range(len(mats)):
                total = jnp.where(kept, 0.0, whole[t])
                for j in range(PIVOTS):
                    total = total - lane_splat(whole[t], first + j) * fresh[t][j]
                done.append(total)
            for t, mat in enumerate(mats):
                mat[...] = done[t]
                for j in range(PIVOTS):
                    mat[pl.ds(first + j, 1), :] = fresh[t][j]
        return carry

    lax.fori_loop(start, stop, group, 0)


def track_flow(fields, east, west, south, north, gains):
    one, two = fields
    gain_e0, gain_e1, gain_w, gain_s0, gain_s1, gain_n0, gain_n1 = gains
    half = one.shape[0]
    middle = gain_e0 * (one - two)
    flow_one = (
        middle
        + gain_w * (one - west)
        + gain_s0 * (one - south[:half])
        + gain_n0 * (one - north[:half])
    )
    flow_two = (
        gain_e1 * (two - east)
        - middle
        + gain_s1 * (two - south[half:])
        + gain_n1 * (two - north[half:])
    )
    return flow_one, flow_two


def column_sum(left, right):
    return jnp.sum(left * right, axis=0, keepdims=True)


def safe_inverse(value):
    return jnp.where(value > 0.0, 1.0 / value, 0.0)


def combination(n):
    up = 1.0 / SCALE
    h00, h01, h02 = n[0] + up * n[1], n[1] + up * n[2], n[2] + up * n[3]
    h11, h12, h22 = h02, n[3] + up * n[4], n[4] + up * n[5]
    inv0 = safe_inverse(h00)
    l10, l20 = h01 * inv0, h02 * inv0
    d11, d12, d22 = h11 - l10 * h01, h12 - l10 * h02, h22 - l20 * h02
    g1, g2 = n[1] - l10 * n[0], n[2] - l20 * n[0]
    inv1 = safe_inverse(d11)
    l21 = d12 * inv1
    c2 = (g2 - l21 * g1) * safe_inverse(d22 - l21 * d12)
    c1 = (g1 - d12 * c2) * inv1
    c0 = (n[0] - h01 * c1 - h02 * c2) * inv0
    return c0, c1, c2


def kernel(
    sizes,
    volt,
    inject,
    conduct,
    cap,
    track,
    driver_tile,
    sink_net,
    sink_count,
    sink_tile,
    sink_node,
    sink_gain,
    out,
    mat0,
    mat1,
    ask,
    asked,
    give,
    given,
    stage0,
    halo0,
    stage,
    halo,
    *rest,
):
    n_row, n_col, rounds = sizes
    reduce_bufs = rest[: len(rounds)]
    ask_send, ask_recv, give_send, give_recv, halo_send, halo_recv, sum_send, sum_recv = rest[len(rounds) :]
    row, col = lax.axis_index("row"), lax.axis_index("col")
    nodes, edge = volt.shape[1], track.shape[1]
    slots = sink_net.shape[0]
    nets = driver_tile.shape[1]
    barrier = pltpu.get_barrier_semaphore()

    def row_peer(i):
        return (lax.rem(row + i, n_row), col)

    def col_peer(i):
        return (row, lax.rem(col + i, n_col))

    def greet(peer):
        def one(i, carry):
            pl.semaphore_signal(barrier, inc=1, device_id=peer(i), device_id_type=MESH)
            return carry

        return one

    lax.fori_loop(1, n_col, greet(col_peer), 0)
    lax.fori_loop(1, n_row, greet(row_peer), 0)

    wanted = sink_net[...].astype(F32)
    for s in range(n_col):
        ask[s * slots : (s + 1) * slots, :] = jnp.broadcast_to(
            wanted[:, s : s + 1], (slots, nodes)
        )
    stage0[0:edge, :] = volt[0, 0:edge, :]
    stage0[edge : 2 * edge, :] = volt[1, 0:edge, :]
    stage0[2 * edge : 2 * edge + 8, :] = jnp.zeros((8, nodes), F32)
    stage0[2 * edge : 2 * edge + 4, 0:edge] = track[...]

    pl.semaphore_wait(barrier, n_col + n_row - 2)

    def send_asks(i, carry):
        peer = col_peer(i)
        pltpu.make_async_remote_copy(
            src_ref=ask.at[pl.ds(pl.multiple_of(peer[1] * slots, slots), slots)],
            dst_ref=asked.at[pl.ds(pl.multiple_of(col * slots, slots), slots)],
            send_sem=ask_send,
            recv_sem=ask_recv,
            device_id=peer,
            device_id_type=MESH,
        ).start()
        return carry

    lax.fori_loop(1, n_col, send_asks, 0)

    neighbours = (col_peer(1), col_peer(n_col - 1), row_peer(1), row_peer(n_row - 1))

    def halo_copy(step, way):
        if step == 0:
            source, target = stage0, halo0.at[way]
        elif way == 0:
            source, target = stage.at[step - 1, 1], halo.at[step - 1, 0, 0]
        elif way == 1:
            source, target = stage.at[step - 1, 0], halo.at[step - 1, 1, 0]
        else:
            source, target = stage.at[step - 1], halo.at[step - 1, way]
        return pltpu.make_async_remote_copy(
            src_ref=source,
            dst_ref=target,
            send_sem=halo_send.at[step, way],
            recv_sem=halo_recv.at[step, way],
            device_id=neighbours[way],
            device_id_type=MESH,
        )

    for way in range(4):
        halo_copy(0, way).start()
    mine = pl.ds(pl.multiple_of(col * slots, slots), slots)
    asked[mine, :] = ask[mine, :]

    r_iota = lax.broadcasted_iota(jnp.int32, (nodes, nodes), 0)
    c_iota = lax.broadcasted_iota(jnp.int32, (nodes, nodes), 1)
    mats = (mat0, mat1)
    for t in range(2):
        mats[t][...] = conduct[t] + jnp.where(r_iota == c_iota, cap[t : t + 1, :], 0.0)
    groups = nodes // 8
    eliminate(mats, 0, groups // 2)

    lanes = lax.broadcasted_iota(jnp.int32, (1, 2 * nets), 1)
    tiles = jnp.concatenate([driver_tile[...], driver_tile[...]], axis=1)
    net_of = jnp.where(lanes >= nets, lanes - nets, lanes)
    tile_of = jnp.where(lanes >= nets, 1, 0)
    code = jnp.where(tiles == tile_of, net_of, -1).astype(F32)
    everything = pl.ds(0, (n_col - 1) * slots)
    pltpu.make_async_copy(asked.at[everything], asked.at[everything], ask_recv).wait()
    pick = jnp.where(asked[...] == code, 1.0, 0.0)
    give[...] = dot(pick, jnp.concatenate([volt[0, 0:nets, :], volt[1, 0:nets, :]], axis=0))

    def send_rows(i, carry):
        peer = col_peer(i)
        pltpu.make_async_remote_copy(
            src_ref=give.at[pl.ds(pl.multiple_of(peer[1] * slots, slots), slots)],
            dst_ref=given.at[pl.ds(pl.multiple_of(col * slots, slots), slots)],
            send_sem=give_send,
            recv_sem=give_recv,
            device_id=peer,
            device_id_type=MESH,
        ).start()
        return carry

    lax.fori_loop(1, n_col, send_rows, 0)
    given[mine, :] = give[mine, :]

    eliminate(mats, groups // 2, groups)

    slot_iota = lax.broadcasted_iota(jnp.int32, (slots, n_col), 0)
    weight = jnp.where(slot_iota < sink_count[...], sink_gain[...], 0.0)
    target = (sink_tile[...] * nodes + sink_node[...]).astype(F32)
    width = n_col * slots
    source = lax.broadcasted_iota(jnp.int32, (n_col, width), 0)
    place = lax.broadcasted_iota(jnp.int32, (n_col, width), 1)
    spread = jnp.where(place // slots == source, 1.0, 0.0)
    flat = dot(jnp.concatenate([target, weight], axis=0), spread)
    place = lax.broadcasted_iota(jnp.int32, (slots, width), 1)
    own = lax.rem(place, slots) == lax.broadcasted_iota(jnp.int32, (slots, width), 0)
    flat_target = jnp.sum(jnp.where(own, flat[:slots], 0.0), axis=0, keepdims=True)
    flat_weight = jnp.sum(jnp.where(own, flat[slots:], 0.0), axis=0, keepdims=True)
    node_row = lax.broadcasted_iota(jnp.int32, (2 * nodes, width), 0).astype(F32)
    scatter = jnp.where(node_row == flat_target, flat_weight, 0.0)

    base = [inject[t] - dot(conduct[t], volt[t]) for t in range(2)]

    for way in range(4):
        halo_copy(0, way).wait_recv()
    eye = lax.broadcasted_iota(jnp.int32, (edge, edge), 0) == lax.broadcasted_iota(
        jnp.int32, (edge, edge), 1
    )
    top = 2 * edge
    lines = [
        track[0:1, :],
        track[2:3, :],
        jnp.where(col == 0, 0.0, halo0[0, top + 2 : top + 3, 0:edge]),
        track[1:2, :],
        track[3:4, :],
        jnp.where(row == 0, 0.0, halo0[2, top + 1 : top + 2, 0:edge]),
        jnp.where(row == 0, 0.0, halo0[2, top + 3 : top + 4, 0:edge]),
    ]
    diagonal = jnp.concatenate([jnp.where(eye, line * SCALE, 0.0) for line in lines], axis=0)
    columns = dot(diagonal, jnp.ones((edge, nodes), F32))
    gains = [columns[i * edge : (i + 1) * edge] for i in range(7)]
    last_col, last_row = col == n_col - 1, row == n_row - 1

    def flow(fields, east, west, south, north):
        east = jnp.where(last_col, 0.0, east)
        south = jnp.where(last_row, 0.0, south)
        return track_flow(fields, east, west, south, north, gains)

    first_flow = flow(
        (volt[0, 0:edge, :], volt[1, 0:edge, :]),
        halo0[1, 0:edge, :],
        halo0[0, edge:top, :],
        halo0[3, 0:top, :],
        halo0[2, 0:top, :],
    )
    pltpu.make_async_copy(given.at[everything], given.at[everything], give_recv).wait()
    current = dot(scatter, given[...])
    resid, guess = [], []
    for t in range(2):
        total = base[t] + current[t * nodes : (t + 1) * nodes]
        total = jnp.concatenate(
            [total[:edge] - first_flow[t] * (1.0 / SCALE), total[edge:]], axis=0
        )
        resid.append(total)
        guess.append(dot(mats[t][...], total))

    moments = []
    fields = [guess[t][:edge] for t in range(2)]
    lifted = []
    for step in (1, 2, 3):
        for t in range(2):
            stage[step - 1, t] = fields[t]
        for way in range(4):
            halo_copy(step, way).start()
        if step == 1:
            moments.append(sum(column_sum(guess[t], resid[t]) for t in range(2)))
        else:
            moments.append(sum(column_sum(fields[t], flows[t]) for t in range(2)))
            lifted.append([dot(mats[t][:, 0:edge], flows[t]) for t in range(2)])
        for way in range(4):
            halo_copy(step, way).wait_recv()
        flows = flow(
            fields,
            halo[step - 1, 1, 0],
            halo[step - 1, 0, 0],
            halo[step - 1, 3].reshape(2 * edge, nodes),
            halo[step - 1, 2].reshape(2 * edge, nodes),
        )
        moments.append(sum(column_sum(fields[t], flows[t]) for t in range(2)))
        if step < 3:
            fields = [dot(mats[t][0:edge, 0:edge], flows[t]) for t in range(2)]

    total = jnp.concatenate(moments + [jnp.zeros((2, nodes), F32)], axis=0)
    for r, (axis, count, stride) in enumerate(rounds):
        buf = reduce_bufs[r]
        position = row if axis == 0 else col
        low = lax.rem(position, stride)
        slot = lax.rem(position // stride, count)
        high = position // (stride * count)
        buf[slot] = total

        def send_sum(i, carry):
            other = high * (stride * count) + lax.rem(slot + i, count) * stride + low
            pltpu.make_async_remote_copy(
                src_ref=buf.at[slot],
                dst_ref=buf.at[slot],
                send_sem=sum_send.at[r],
                recv_sem=sum_recv.at[r],
                device_id=(other, col) if axis == 0 else (row, other),
                device_id_type=MESH,
            ).start()
            return carry

        lax.fori_loop(1, count, send_sum, 0)
        pltpu.make_async_copy(
            buf.at[pl.ds(0, count - 1)], buf.at[pl.ds(0, count - 1)], sum_recv.at[r]
        ).wait()
        parts = [buf[i] for i in range(count)]
        while len(parts) > 1:
            pairs = [parts[i] + parts[i + 1] for i in range(0, len(parts) - 1, 2)]
            parts = pairs + ([parts[-1]] if len(parts) % 2 else [])
        total = parts[0]

    c0, c1, c2 = combination([total[i : i + 1] for i in range(6)])
    for t in range(2):
        out[t] = volt[t] + c0 * guess[t] + c1 * lifted[0][t] + c2 * lifted[1][t]

    for step in range(4):
        for way in range(4):
            halo_copy(step, way).wait_send()
    pltpu.make_async_copy(ask.at[everything], ask.at[everything], ask_send).wait()
    pltpu.make_async_copy(give.at[everything], give.at[everything], give_send).wait()
    for r, (axis, count, stride) in enumerate(rounds):
        part = reduce_bufs[r].at[pl.ds(0, count - 1)]
        pltpu.make_async_copy(part, part, sum_send.at[r]).wait()


def local(
    initial_voltage,
    inject,
    conduct,
    capacitance,
    track_gain,
    driver_tile,
    sink_net,
    sink_count,
    sink_tile,
    sink_node,
    sink_gain,
):
    n_row, n_col = lax.axis_size("row"), lax.axis_size("col")
    tiles, nodes, patterns = initial_voltage.shape[1:]
    edge = track_gain.shape[-1]
    slots = sink_net.shape[-1]
    rounds = ((0, n_row, 1), (1, 4, 1), (1, n_col // 4, 4))

    def by_slot(array):
        return jnp.swapaxes(array.reshape(n_col, slots), 0, 1)

    block = (tiles, nodes, patterns)
    vmem = pl.BlockSpec(memory_space=pltpu.VMEM)
    result = pl.pallas_call(
        functools.partial(kernel, (n_row, n_col, rounds)),
        out_shape=jax.ShapeDtypeStruct(block, F32),
        in_specs=[vmem] * 11,
        out_specs=vmem,
        scratch_shapes=[
            pltpu.VMEM((nodes, nodes), F32),
            pltpu.VMEM((nodes, nodes), F32),
            pltpu.VMEM((n_col * slots, patterns), F32),
            pltpu.VMEM((n_col * slots, patterns), F32),
            pltpu.VMEM((n_col * slots, patterns), F32),
            pltpu.VMEM((n_col * slots, patterns), F32),
            pltpu.VMEM((2 * edge + 8, patterns), F32),
            pltpu.VMEM((4, 2 * edge + 8, patterns), F32),
            pltpu.VMEM((3, 2, edge, patterns), F32),
            pltpu.VMEM((3, 4, 2, edge, patterns), F32),
            *[pltpu.VMEM((count, 8, patterns), F32) for _, count, _ in rounds],
            pltpu.SemaphoreType.DMA,
            pltpu.SemaphoreType.DMA,
            pltpu.SemaphoreType.DMA,
            pltpu.SemaphoreType.DMA,
            pltpu.SemaphoreType.DMA((4, 4)),
            pltpu.SemaphoreType.DMA((4, 4)),
            pltpu.SemaphoreType.DMA((len(rounds),)),
            pltpu.SemaphoreType.DMA((len(rounds),)),
        ],
        compiler_params=pltpu.CompilerParams(collective_id=0, has_side_effects=True),
        name="transient",
    )(
        initial_voltage.reshape(block),
        inject.reshape(block),
        conduct.reshape(block),
        capacitance.reshape(tiles, nodes),
        track_gain.reshape(2 * tiles, edge),
        driver_tile.reshape(1, -1),
        by_slot(sink_net),
        sink_count.reshape(1, n_col),
        by_slot(sink_tile),
        by_slot(sink_node),
        by_slot(sink_gain),
    )
    return result.reshape(initial_voltage.shape)


def solution(mesh):
    four = P("row", "col", None, None)
    three = P("row", "col", None)
    placed = (four, four, four, three, four, three, four, three, four, four, four)
    return jax.shard_map(local, mesh=mesh, in_specs=placed, out_specs=four, check_vma=False)
```

```python
import functools

import jax
import jax.numpy as jnp
from jax import lax
from jax.experimental import pallas as pl
from jax.experimental.pallas import tpu as pltpu
from jax.sharding import PartitionSpec as P

F32 = jnp.float32
HIGH = lax.Precision.HIGHEST
MESH = pl.DeviceIdType.MESH
SCALE = 1.0 / 32.0
PIVOTS = 4
DEPTH = 3


def dot(left, right):
    return jnp.dot(left, right, precision=HIGH, preferred_element_type=F32)


def lane_splat(block, lane):
    return jnp.take_along_axis(block, jnp.full(block.shape, lane, jnp.int32), axis=1)


def pivot_rows(rows, first, offset, lane):
    mine = [rows[offset + i : offset + i + 1] for i in range(PIVOTS)]
    splats = [lane_splat(rows, first + j) for j in range(PIVOTS)]
    small = [
        [splats[j][offset + i : offset + i + 1] for j in range(PIVOTS)]
        for i in range(PIVOTS)
    ]
    for j in range(PIVOTS):
        scale = 1.0 / small[j][j]
        row = [scale if m == j else small[j][m] * scale for m in range(PIVOTS)]
        for i in range(PIVOTS):
            if i == j:
                continue
            factor = small[i][j]
            small[i] = [
                -factor * scale if m == j else small[i][m] - factor * row[m]
                for m in range(PIVOTS)
            ]
        small[j] = row
    fresh = []
    for i in range(PIVOTS):
        total = small[i][0] * mine[0]
        for j in range(1, PIVOTS):
            total = total + small[i][j] * mine[j]
        for j in range(PIVOTS):
            total = jnp.where(lane == first + j, small[i][j], total)
        fresh.append(total)
    return fresh


def eliminate(mats, start, stop):
    nodes = mats[0].shape[0]
    lane = lax.broadcasted_iota(jnp.int32, (1, nodes), 1)

    def group(index, carry):
        base = pl.multiple_of(index * 8, 8)
        for offset in range(0, 8, PIVOTS):
            first = base + offset
            whole = [mat[...] for mat in mats]
            rows = [mat[pl.ds(base, 8), :] for mat in mats]
            fresh = [pivot_rows(r, first, offset, lane) for r in rows]
            kept = (lane >= first) & (lane < first + PIVOTS)
            done = []
            for t in range(len(mats)):
                total = jnp.where(kept, 0.0, whole[t])
                for j in range(PIVOTS):
                    total = total - lane_splat(whole[t], first + j) * fresh[t][j]
                done.append(total)
            for t, mat in enumerate(mats):
                mat[...] = done[t]
                for j in range(PIVOTS):
                    mat[pl.ds(first + j, 1), :] = fresh[t][j]
        return carry

    lax.fori_loop(start, stop, group, 0)


def ring_peers(position, high_count, low_count):
    high, low = position // low_count, lax.rem(position, low_count)
    offsets = [(a, b) for a in range(high_count) for b in range(low_count) if a or b]
    offsets.sort(key=lambda o: -(min(o[0], high_count - o[0]) + min(o[1], low_count - o[1])))
    return [
        lax.rem(high + a, high_count) * low_count + lax.rem(low + b, low_count)
        for a, b in offsets
    ]


def near(depth):
    span = range(-depth - 1, depth + 3)
    return [
        (r, c) for r in span for c in span if abs(r) + max(-c, 0, c - 1) <= depth
    ]


def from_devices(tiles):
    held = {}
    for r, c in tiles:
        held.setdefault((r, c // 2), []).append(c % 2)
    held.pop((0, 0), None)
    far = lambda o: -(2 * abs(o[1]) + abs(o[0]))
    return {o: sorted(held[o]) for o in sorted(held, key=far)}


def gain_lines(depth):
    east, south = [], []
    for r, c in near(depth):
        east += [(r, c), (r, c - 1)]
        south += [(r, c), (r - 1, c)]
    return [(0, t) for t in dict.fromkeys(east)] + [(1, t) for t in dict.fromkeys(south)]


def column_sum(left, right):
    return jnp.sum(left * right, axis=0, keepdims=True)


def safe_inverse(value):
    return jnp.where(value > 0.0, 1.0 / value, 0.0)


def combination(n):
    up = 1.0 / SCALE
    h00, h01, h02 = n[0] + up * n[1], n[1] + up * n[2], n[2] + up * n[3]
    h11, h12, h22 = h02, n[3] + up * n[4], n[4] + up * n[5]
    inv0 = safe_inverse(h00)
    l10, l20 = h01 * inv0, h02 * inv0
    d11, d12, d22 = h11 - l10 * h01, h12 - l10 * h02, h22 - l20 * h02
    g1, g2 = n[1] - l10 * n[0], n[2] - l20 * n[0]
    inv1 = safe_inverse(d11)
    l21 = d12 * inv1
    c2 = (g2 - l21 * g1) * safe_inverse(d22 - l21 * d12)
    c1 = (g1 - d12 * c2) * inv1
    c0 = (n[0] - h01 * c1 - h02 * c2) * inv0
    return c0, c1, c2


def kernel(
    sizes,
    volt_hbm,
    inject_hbm,
    conduct_hbm,
    cap_hbm,
    track_hbm,
    driver_tile_hbm,
    sink_net_hbm,
    sink_count_hbm,
    sink_tile_hbm,
    sink_node_hbm,
    sink_gain_hbm,
    out,
    volt,
    inject,
    conduct,
    cap,
    track,
    driver_tile,
    sink_net,
    sink_count,
    sink_tile,
    sink_node,
    sink_gain,
    mat0,
    mat1,
    ask,
    asked,
    give,
    given,
    lines,
    lines_in,
    start_in,
    block_in,
    rims,
    rims_in,
    late,
    late_in,
    row_sums,
    col_sums,
    load_sem,
    ask_send,
    ask_recv,
    give_send,
    give_recv,
    lines_send,
    lines_recv,
    start_send,
    start_recv,
    block_send,
    block_recv,
    rims_send,
    rims_recv,
    late_send,
    late_recv,
    sum_send,
    sum_recv,
):
    n_row, n_col = sizes
    row, col = lax.axis_index("row"), lax.axis_index("col")
    nodes, edge = volt.shape[1], track.shape[1]
    slots = sink_net.shape[0]
    nets = driver_tile.shape[1]

    loads = [
        pltpu.make_async_copy(source, target, load_sem.at[i])
        for i, (source, target) in enumerate(
            (
                (sink_net_hbm, sink_net),
                (track_hbm, track),
                (volt_hbm, volt),
                (cap_hbm, cap),
                (conduct_hbm, conduct),
                (driver_tile_hbm, driver_tile),
                (sink_count_hbm, sink_count),
                (sink_tile_hbm, sink_tile),
                (sink_node_hbm, sink_node),
                (sink_gain_hbm, sink_gain),
                (inject_hbm, inject),
            )
        )
    ]
    for load in loads:
        load.start()

    row_group = [(position, col) for position in ring_peers(row, n_row // 2, 2)]
    col_group = [(row, position) for position in ring_peers(col, n_col // 4, 4)]
    wide = from_devices(near(DEPTH))
    blocks = from_devices(near(DEPTH - 1))
    tracks = from_devices([tile for _, tile in gain_lines(DEPTH - 1)])
    sides = from_devices(near(1))

    def device(offset):
        r, c = offset
        return (lax.rem(row + (n_row + r), n_row), lax.rem(col + (n_col + c), n_col))

    def back(offset):
        return device((-offset[0], -offset[1]))

    corners = [device(o) for o in wide if o[0] and o[1]]
    barrier = pltpu.get_barrier_semaphore()
    for peer in col_group + row_group + corners:
        pl.semaphore_signal(barrier, inc=1, device_id=peer, device_id_type=MESH)

    loads[0].wait()
    wanted = sink_net[...].astype(F32)
    for s in range(n_col):
        ask[s * slots : (s + 1) * slots, :] = jnp.broadcast_to(
            wanted[:, s : s + 1], (slots, nodes)
        )
    loads[1].wait()
    lines[...] = jnp.zeros(lines.shape, F32)
    lines[0:4, 0:edge] = track[...]
    loads[2].wait()

    pl.semaphore_wait(barrier, len(col_group) + len(row_group) + len(corners))

    def slot_rows(position):
        return pl.ds(pl.multiple_of(position * slots, slots), slots)

    def exchange(source, target, send, recv):
        for peer in col_group:
            pltpu.make_async_remote_copy(
                src_ref=source.at[slot_rows(peer[1])],
                dst_ref=target.at[slot_rows(col)],
                send_sem=send,
                recv_sem=recv,
                device_id=peer,
                device_id_type=MESH,
            ).start()

    def tile_part(ref, tiles):
        return ref if len(tiles) == 2 else ref.at[tiles[0]]

    def copies(sources, targets, users, send, recv):
        return [
            pltpu.make_async_remote_copy(
                src_ref=tile_part(sources, tiles),
                dst_ref=tile_part(targets.at[i], tiles),
                send_sem=send.at[i],
                recv_sem=recv.at[i],
                device_id=back(offset),
                device_id_type=MESH,
            )
            for i, (offset, tiles) in enumerate(users.items())
        ]

    exchange(ask, asked, ask_send, ask_recv)
    line_copies = [
        pltpu.make_async_remote_copy(
            src_ref=lines,
            dst_ref=lines_in.at[i],
            send_sem=lines_send.at[i],
            recv_sem=lines_recv.at[i],
            device_id=back(offset),
            device_id_type=MESH,
        )
        for i, offset in enumerate(tracks)
    ]
    start_copies = copies(volt.at[:, pl.ds(0, edge)], start_in, sides, start_send, start_recv)
    for copy in line_copies + start_copies:
        copy.start()
    asked[slot_rows(col), :] = ask[slot_rows(col), :]

    loads[3].wait()
    loads[4].wait()
    r_iota = lax.broadcasted_iota(jnp.int32, (nodes, nodes), 0)
    c_iota = lax.broadcasted_iota(jnp.int32, (nodes, nodes), 1)
    mats = (mat0, mat1)
    for t in range(2):
        mats[t][...] = conduct[t] + jnp.where(r_iota == c_iota, cap[t : t + 1, :], 0.0)
    groups = nodes // 8
    eliminate(mats, 0, groups // 2)

    loads[5].wait()
    lanes = lax.broadcasted_iota(jnp.int32, (1, 2 * nets), 1)
    tiles = jnp.concatenate([driver_tile[...], driver_tile[...]], axis=1)
    net_of = jnp.where(lanes >= nets, lanes - nets, lanes)
    tile_of = jnp.where(lanes >= nets, 1, 0)
    code = jnp.where(tiles == tile_of, net_of, -1).astype(F32)
    everything = pl.ds(0, (n_col - 1) * slots)
    pltpu.make_async_copy(asked.at[everything], asked.at[everything], ask_recv).wait()
    pick = jnp.where(asked[...] == code, 1.0, 0.0)
    give[...] = dot(pick, jnp.concatenate([volt[0, 0:nets, :], volt[1, 0:nets, :]], axis=0))
    exchange(give, given, give_send, give_recv)
    given[slot_rows(col), :] = give[slot_rows(col), :]

    eliminate(mats, groups // 2, groups)
    block_copies = []
    for i, (offset, held) in enumerate(blocks.items()):
        for t in held:
            block_copies.append(
                pltpu.make_async_remote_copy(
                    src_ref=mats[t].at[pl.ds(0, edge)],
                    dst_ref=block_in.at[i, t],
                    send_sem=block_send.at[i, t],
                    recv_sem=block_recv.at[i, t],
                    device_id=back(offset),
                    device_id_type=MESH,
                )
            )
    for copy in block_copies:
        copy.start()

    for load in loads[6:]:
        load.wait()
    slot_iota = lax.broadcasted_iota(jnp.int32, (slots, n_col), 0)
    weight = jnp.where(slot_iota < sink_count[...], sink_gain[...], 0.0)
    target = (sink_tile[...] * nodes + sink_node[...]).astype(F32)
    width = n_col * slots
    source = lax.broadcasted_iota(jnp.int32, (n_col, width), 0)
    place = lax.broadcasted_iota(jnp.int32, (n_col, width), 1)
    spread = jnp.where(place // slots == source, 1.0, 0.0)
    flat = dot(jnp.concatenate([target, weight], axis=0), spread)
    place = lax.broadcasted_iota(jnp.int32, (slots, width), 1)
    own = lax.rem(place, slots) == lax.broadcasted_iota(jnp.int32, (slots, width), 0)
    flat_target = jnp.sum(jnp.where(own, flat[:slots], 0.0), axis=0, keepdims=True)
    flat_weight = jnp.sum(jnp.where(own, flat[slots:], 0.0), axis=0, keepdims=True)
    node_row = lax.broadcasted_iota(jnp.int32, (2 * nodes, width), 0).astype(F32)
    scatter = jnp.where(node_row == flat_target, flat_weight, 0.0)

    base = [inject[t] - dot(conduct[t], volt[t]) for t in range(2)]

    def inside(offset):
        r, c = offset
        at_row, at_col = row + r, col + c
        return (at_row >= 0) & (at_row < n_row) & (at_col >= 0) & (at_col < n_col)

    present = {o: inside(o) for o in {**wide, **tracks}}

    def home(tile):
        return (tile[0], tile[1] // 2), tile[1] % 2

    def only_inside(tile, value):
        offset = home(tile)[0]
        return value if offset == (0, 0) else jnp.where(present[offset], value, 0.0)

    for copy in line_copies:
        copy.wait_recv()
    eye = lax.broadcasted_iota(jnp.int32, (edge, edge), 0) == lax.broadcasted_iota(
        jnp.int32, (edge, edge), 1
    )
    names = gain_lines(DEPTH - 1)
    place_of = {o: i for i, o in enumerate(tracks)}
    diagonals = []
    for way, tile in names:
        offset, t = home(tile)
        at = 2 * t + way
        if offset == (0, 0):
            line = track[at : at + 1, :]
        else:
            line = lines_in[place_of[offset], at : at + 1, 0:edge]
        diagonals.append(jnp.where(eye, only_inside(tile, line) * SCALE, 0.0))
    columns = dot(jnp.concatenate(diagonals, axis=0), jnp.ones((edge, nodes), F32))
    gains = {name: columns[i * edge : (i + 1) * edge] for i, name in enumerate(names)}

    def flow(tile, field):
        r, c = tile
        v = field[tile]
        total = gains[0, (r, c)] * (v - field[r, c + 1])
        total = total + gains[0, (r, c - 1)] * (v - field[r, c - 1])
        total = total + gains[1, (r, c)] * (v - field[r + 1, c])
        return total + gains[1, (r - 1, c)] * (v - field[r - 1, c])

    def gathered(depth, received, users, mine):
        field = {(0, t): mine[t] for t in range(2)}
        where = {o: i for i, o in enumerate(users)}
        for tile in near(depth):
            offset, t = home(tile)
            if offset != (0, 0):
                field[tile] = only_inside(tile, received[where[offset], t])
        return field

    own_tiles = ((0, 0), (0, 1))
    for copy in start_copies:
        copy.wait_recv()
    start = gathered(1, start_in, sides, [volt[t, 0:edge, :] for t in range(2)])
    first_flow = [flow(tile, start) for tile in own_tiles]
    pltpu.make_async_copy(given.at[everything], given.at[everything], give_recv).wait()
    current = dot(scatter, given[...])
    resid, guess = [], []
    for t in range(2):
        total = base[t] + current[t * nodes : (t + 1) * nodes]
        total = jnp.concatenate(
            [total[:edge] - first_flow[t] * (1.0 / SCALE), total[edge:]], axis=0
        )
        resid.append(total)
        guess.append(dot(mats[t][...], total))
        rims[t] = guess[t][:edge]

    rim_copies = copies(rims, rims_in, wide, rims_send, rims_recv)
    for copy in rim_copies:
        copy.start()
    moments = [sum(column_sum(guess[t], resid[t]) for t in range(2))]
    for copy in block_copies:
        copy.wait_recv()
    block = {(0, t): mats[t][0:edge, 0:edge] for t in range(2)}
    block_at = {o: i for i, o in enumerate(blocks)}
    for tile in near(DEPTH - 1):
        offset, t = home(tile)
        if offset != (0, 0):
            block[tile] = block_in[block_at[offset], t, :, 0:edge]
    for copy in rim_copies:
        copy.wait_recv()

    field = gathered(DEPTH, rims_in, wide, [guess[t][:edge] for t in range(2)])
    lifted, late_copies = [], []
    for step in range(3):
        reach = DEPTH - 1 - step
        if reach < 0:
            for t in range(2):
                late[t] = field[0, t]
            late_copies = copies(late, late_in, sides, late_send, late_recv)
            for copy in late_copies:
                copy.start()
            lifted.append([dot(mats[t][:, 0:edge], flows[0, t]) for t in range(2)])
            for copy in late_copies:
                copy.wait_recv()
            field = gathered(1, late_in, sides, [field[0, t] for t in range(2)])
            reach = 0
        flows = {tile: flow(tile, field) for tile in near(reach)}
        moments.append(sum(column_sum(field[0, t], flows[0, t]) for t in range(2)))
        if step < 2:
            if reach or DEPTH > 2:
                lifted.append([dot(mats[t][:, 0:edge], flows[0, t]) for t in range(2)])
            field = {
                tile: only_inside(tile, dot(block[tile], flows[tile])) for tile in near(reach)
            }
            moments.append(sum(column_sum(field[0, t], flows[0, t]) for t in range(2)))

    total = jnp.concatenate(moments + [jnp.zeros((2, nodes), F32)], axis=0)
    for r, (slot, group) in enumerate(((row, row_group), (col, col_group))):
        buf, count = (row_sums, col_sums)[r], len(group) + 1
        buf[slot] = total
        for peer in group:
            pltpu.make_async_remote_copy(
                src_ref=buf.at[slot],
                dst_ref=buf.at[slot],
                send_sem=sum_send.at[r],
                recv_sem=sum_recv.at[r],
                device_id=peer,
                device_id_type=MESH,
            ).start()
        part = buf.at[pl.ds(0, count - 1)]
        pltpu.make_async_copy(part, part, sum_recv.at[r]).wait()
        parts = [buf[i] for i in range(count)]
        while len(parts) > 1:
            pairs = [parts[i] + parts[i + 1] for i in range(0, len(parts) - 1, 2)]
            parts = pairs + ([parts[-1]] if len(parts) % 2 else [])
        total = parts[0]

    c0, c1, c2 = combination([total[i : i + 1] for i in range(6)])
    for t in range(2):
        out[t] = c0 * guess[t] + c1 * lifted[0][t] + c2 * lifted[1][t]

    for copy in line_copies + start_copies + block_copies + rim_copies + late_copies:
        copy.wait_send()
    pltpu.make_async_copy(ask.at[everything], ask.at[everything], ask_send).wait()
    pltpu.make_async_copy(give.at[everything], give.at[everything], give_send).wait()
    for r, group in enumerate((row_group, col_group)):
        part = (row_sums, col_sums)[r].at[pl.ds(0, len(group))]
        pltpu.make_async_copy(part, part, sum_send.at[r]).wait()


def local(
    initial_voltage,
    inject,
    conduct,
    capacitance,
    track_gain,
    driver_tile,
    sink_net,
    sink_count,
    sink_tile,
    sink_node,
    sink_gain,
):
    n_row, n_col = lax.axis_size("row"), lax.axis_size("col")
    tiles, nodes, patterns = initial_voltage.shape[1:]
    edge = track_gain.shape[-1]
    slots = sink_net.shape[-1]

    def by_slot(array):
        return jnp.swapaxes(array.reshape(n_col, slots), 0, 1)

    block = (tiles, nodes, patterns)
    arrays = (
        initial_voltage.reshape(block),
        inject.reshape(block),
        conduct.reshape(block),
        capacitance.reshape(tiles, nodes),
        track_gain.reshape(2 * tiles, edge),
        driver_tile.reshape(1, -1),
        by_slot(sink_net),
        sink_count.reshape(1, n_col),
        by_slot(sink_tile),
        by_slot(sink_node),
        by_slot(sink_gain),
    )
    rim = (tiles, edge, patterns)
    wide, blocks = from_devices(near(DEPTH)), from_devices(near(DEPTH - 1))
    tracks = from_devices([tile for _, tile in gain_lines(DEPTH - 1)])
    dma = pltpu.SemaphoreType.DMA
    slot_rows = pltpu.VMEM((n_col * slots, patterns), F32)
    result = pl.pallas_call(
        functools.partial(kernel, (n_row, n_col)),
        out_shape=jax.ShapeDtypeStruct(block, F32),
        in_specs=[pl.BlockSpec(memory_space=pltpu.HBM)] * len(arrays),
        out_specs=pl.BlockSpec(memory_space=pltpu.VMEM),
        scratch_shapes=[
            *[pltpu.VMEM(array.shape, array.dtype) for array in arrays],
            pltpu.VMEM((nodes, nodes), F32),
            pltpu.VMEM((nodes, nodes), F32),
            *[slot_rows] * 4,
            pltpu.VMEM((8, patterns), F32),
            pltpu.VMEM((len(tracks), 8, patterns), F32),
            pltpu.VMEM((4, *rim), F32),
            pltpu.VMEM((len(blocks), *rim), F32),
            pltpu.VMEM(rim, F32),
            pltpu.VMEM((len(wide), *rim), F32),
            pltpu.VMEM(rim, F32),
            pltpu.VMEM((4, *rim), F32),
            pltpu.VMEM((n_row, 8, patterns), F32),
            pltpu.VMEM((n_col, 8, patterns), F32),
            dma((len(arrays),)),
            *[dma] * 4,
            *[dma((len(tracks),))] * 2,
            *[dma((4,))] * 2,
            *[dma((len(blocks), tiles))] * 2,
            *[dma((len(wide),))] * 2,
            *[dma((4,))] * 2,
            *[dma((2,))] * 2,
        ],
        compiler_params=pltpu.CompilerParams(
            collective_id=0, has_side_effects=True
        ),
        name="transient",
    )(*arrays)
    return initial_voltage + result.reshape(initial_voltage.shape)


def solution(mesh):
    four = P("row", "col", None, None)
    three = P("row", "col", None)
    placed = (four, four, four, three, four, three, four, three, four, four, four)
    return jax.shard_map(local, mesh=mesh, in_specs=placed, out_specs=four, check_vma=False)
```

```python
import functools

import jax
import jax.numpy as jnp
from jax import lax
from jax.experimental import pallas as pl
from jax.experimental.pallas import tpu as pltpu
from jax.sharding import PartitionSpec as P

F32 = jnp.float32
HIGH = lax.Precision.HIGHEST
MESH = pl.DeviceIdType.MESH
SCALE = 1.0 / 32.0
PIVOTS = 4
DEPTH = 3


def dot(left, right):
    return jnp.dot(left, right, precision=HIGH, preferred_element_type=F32)


def lane_splat(block, lane):
    return jnp.take_along_axis(block, jnp.full(block.shape, lane, jnp.int32), axis=1)


def pivot_rows(rows, first, offset, lane):
    mine = [rows[offset + i : offset + i + 1] for i in range(PIVOTS)]
    splats = [lane_splat(rows, first + j) for j in range(PIVOTS)]
    small = [
        [splats[j][offset + i : offset + i + 1] for j in range(PIVOTS)]
        for i in range(PIVOTS)
    ]
    for j in range(PIVOTS):
        scale = 1.0 / small[j][j]
        row = [scale if m == j else small[j][m] * scale for m in range(PIVOTS)]
        for i in range(PIVOTS):
            if i == j:
                continue
            factor = small[i][j]
            small[i] = [
                -factor * scale if m == j else small[i][m] - factor * row[m]
                for m in range(PIVOTS)
            ]
        small[j] = row
    fresh = []
    for i in range(PIVOTS):
        total = small[i][0] * mine[0]
        for j in range(1, PIVOTS):
            total = total + small[i][j] * mine[j]
        for j in range(PIVOTS):
            total = jnp.where(lane == first + j, small[i][j], total)
        fresh.append(total)
    return fresh


def eliminate(mats, start, stop):
    nodes = mats[0].shape[0]
    lane = lax.broadcasted_iota(jnp.int32, (1, nodes), 1)

    def group(index, carry):
        base = pl.multiple_of(index * 8, 8)
        for offset in range(0, 8, PIVOTS):
            first = base + offset
            whole = [mat[...] for mat in mats]
            rows = [mat[pl.ds(base, 8), :] for mat in mats]
            fresh = [pivot_rows(r, first, offset, lane) for r in rows]
            kept = (lane >= first) & (lane < first + PIVOTS)
            done = []
            for t in range(len(mats)):
                total = jnp.where(kept, 0.0, whole[t])
                for j in range(PIVOTS):
                    total = total - lane_splat(whole[t], first + j) * fresh[t][j]
                done.append(total)
            for t, mat in enumerate(mats):
                mat[...] = done[t]
                for j in range(PIVOTS):
                    mat[pl.ds(first + j, 1), :] = fresh[t][j]
        return carry

    lax.fori_loop(start, stop, group, 0)


def ring_peers(position, high_count, low_count):
    high, low = position // low_count, lax.rem(position, low_count)
    offsets = [(a, b) for a in range(high_count) for b in range(low_count) if a or b]
    offsets.sort(key=lambda o: -(min(o[0], high_count - o[0]) + min(o[1], low_count - o[1])))
    return [
        lax.rem(high + a, high_count) * low_count + lax.rem(low + b, low_count)
        for a, b in offsets
    ]


def near(depth):
    span = range(-depth - 1, depth + 3)
    return [
        (r, c) for r in span for c in span if abs(r) + max(-c, 0, c - 1) <= depth
    ]


def from_devices(tiles):
    held = {}
    for r, c in tiles:
        held.setdefault((r, c // 2), []).append(c % 2)
    held.pop((0, 0), None)
    far = lambda o: -(2 * abs(o[1]) + abs(o[0]))
    return {o: sorted(held[o]) for o in sorted(held, key=far)}


def gain_lines(depth):
    east, south = [], []
    for r, c in near(depth):
        east += [(r, c), (r, c - 1)]
        south += [(r, c), (r - 1, c)]
    return [(0, t) for t in dict.fromkeys(east)] + [(1, t) for t in dict.fromkeys(south)]


def column_sum(left, right):
    return jnp.sum(left * right, axis=0, keepdims=True)


def safe_inverse(value):
    return jnp.where(value > 0.0, 1.0 / value, 0.0)


def combination(n):
    up = 1.0 / SCALE
    h00, h01, h02 = n[0] + up * n[1], n[1] + up * n[2], n[2] + up * n[3]
    h11, h12, h22 = h02, n[3] + up * n[4], n[4] + up * n[5]
    inv0 = safe_inverse(h00)
    l10, l20 = h01 * inv0, h02 * inv0
    d11, d12, d22 = h11 - l10 * h01, h12 - l10 * h02, h22 - l20 * h02
    g1, g2 = n[1] - l10 * n[0], n[2] - l20 * n[0]
    inv1 = safe_inverse(d11)
    l21 = d12 * inv1
    c2 = (g2 - l21 * g1) * safe_inverse(d22 - l21 * d12)
    c1 = (g1 - d12 * c2) * inv1
    c0 = (n[0] - h01 * c1 - h02 * c2) * inv0
    return c0, c1, c2


def kernel(
    sizes,
    volt_hbm,
    inject_hbm,
    conduct_hbm,
    cap_hbm,
    track_hbm,
    driver_tile_hbm,
    sink_net_hbm,
    sink_count_hbm,
    sink_tile_hbm,
    sink_node_hbm,
    sink_gain_hbm,
    out,
    volt,
    inject,
    conduct,
    cap,
    track,
    driver_tile,
    sink_net,
    sink_count,
    sink_tile,
    sink_node,
    sink_gain,
    mat0,
    mat1,
    ask,
    asked,
    give,
    given,
    lines,
    lines_in,
    start_in,
    block_in,
    rims,
    rims_in,
    late,
    late_in,
    row_sums,
    col_sums,
    load_sem,
    ask_send,
    ask_recv,
    give_send,
    give_recv,
    lines_send,
    lines_recv,
    start_send,
    start_recv,
    block_send,
    block_recv,
    rims_send,
    rims_recv,
    late_send,
    late_recv,
    sum_send,
    sum_recv,
):
    n_row, n_col = sizes
    row, col = lax.axis_index("row"), lax.axis_index("col")
    nodes, edge = volt.shape[1], track.shape[1]
    slots = sink_net.shape[0]
    nets = driver_tile.shape[1]

    loads = [
        pltpu.make_async_copy(source, target, load_sem.at[i])
        for i, (source, target) in enumerate(
            (
                (sink_net_hbm, sink_net),
                (track_hbm, track),
                (volt_hbm, volt),
                (cap_hbm, cap),
                (conduct_hbm, conduct),
                (driver_tile_hbm, driver_tile),
                (sink_count_hbm, sink_count),
                (sink_tile_hbm, sink_tile),
                (sink_node_hbm, sink_node),
                (sink_gain_hbm, sink_gain),
                (inject_hbm, inject),
            )
        )
    ]
    for load in loads:
        load.start()

    row_group = [(position, col) for position in ring_peers(row, n_row // 2, 2)]
    col_group = [(row, position) for position in ring_peers(col, n_col // 4, 4)]
    wide = from_devices(near(DEPTH))
    blocks = from_devices(near(DEPTH - 1))
    tracks = from_devices([tile for _, tile in gain_lines(DEPTH - 1)])
    sides = from_devices(near(1))

    def device(offset):
        r, c = offset
        return (lax.rem(row + (n_row + r), n_row), lax.rem(col + (n_col + c), n_col))

    def back(offset):
        return device((-offset[0], -offset[1]))

    corners = [device(o) for o in wide if o[0] and o[1]]
    barrier = pltpu.get_barrier_semaphore()
    for peer in col_group + row_group + corners:
        pl.semaphore_signal(barrier, inc=1, device_id=peer, device_id_type=MESH)

    loads[0].wait()
    wanted = sink_net[...].astype(F32)
    for s in range(n_col):
        ask[s * slots : (s + 1) * slots, :] = jnp.broadcast_to(
            wanted[:, s : s + 1], (slots, nodes)
        )
    loads[1].wait()
    lines[...] = jnp.zeros(lines.shape, F32)
    lines[0:4, 0:edge] = track[...]
    loads[2].wait()

    pl.semaphore_wait(barrier, len(col_group) + len(row_group) + len(corners))

    def slot_rows(position):
        return pl.ds(pl.multiple_of(position * slots, slots), slots)

    def exchange(source, target, send, recv):
        for peer in col_group:
            pltpu.make_async_remote_copy(
                src_ref=source.at[slot_rows(peer[1])],
                dst_ref=target.at[slot_rows(col)],
                send_sem=send,
                recv_sem=recv,
                device_id=peer,
                device_id_type=MESH,
            ).start()

    def tile_part(ref, tiles):
        return ref if len(tiles) == 2 else ref.at[tiles[0]]

    def copies(sources, targets, users, send, recv):
        return [
            pltpu.make_async_remote_copy(
                src_ref=tile_part(sources, tiles),
                dst_ref=tile_part(targets.at[i], tiles),
                send_sem=send.at[i],
                recv_sem=recv.at[i],
                device_id=back(offset),
                device_id_type=MESH,
            )
            for i, (offset, tiles) in enumerate(users.items())
        ]

    exchange(ask, asked, ask_send, ask_recv)
    line_copies = [
        pltpu.make_async_remote_copy(
            src_ref=lines,
            dst_ref=lines_in.at[i],
            send_sem=lines_send.at[i],
            recv_sem=lines_recv.at[i],
            device_id=back(offset),
            device_id_type=MESH,
        )
        for i, offset in enumerate(tracks)
    ]
    start_copies = copies(volt.at[:, pl.ds(0, edge)], start_in, sides, start_send, start_recv)
    for copy in line_copies + start_copies:
        copy.start()
    asked[slot_rows(col), :] = ask[slot_rows(col), :]

    loads[3].wait()
    loads[4].wait()
    r_iota = lax.broadcasted_iota(jnp.int32, (nodes, nodes), 0)
    c_iota = lax.broadcasted_iota(jnp.int32, (nodes, nodes), 1)
    mats = (mat0, mat1)
    for t in range(2):
        mats[t][...] = conduct[t] + jnp.where(r_iota == c_iota, cap[t : t + 1, :], 0.0)
    groups = nodes // 8
    eliminate(mats, 0, groups // 2)

    loads[5].wait()
    lanes = lax.broadcasted_iota(jnp.int32, (1, 2 * nets), 1)
    tiles = jnp.concatenate([driver_tile[...], driver_tile[...]], axis=1)
    net_of = jnp.where(lanes >= nets, lanes - nets, lanes)
    tile_of = jnp.where(lanes >= nets, 1, 0)
    code = jnp.where(tiles == tile_of, net_of, -1).astype(F32)
    everything = pl.ds(0, (n_col - 1) * slots)
    pltpu.make_async_copy(asked.at[everything], asked.at[everything], ask_recv).wait()
    pick = jnp.where(asked[...] == code, 1.0, 0.0)
    give[...] = dot(pick, jnp.concatenate([volt[0, 0:nets, :], volt[1, 0:nets, :]], axis=0))
    exchange(give, given, give_send, give_recv)
    given[slot_rows(col), :] = give[slot_rows(col), :]

    eliminate(mats, groups // 2, groups)
    block_copies = []
    for i, (offset, held) in enumerate(blocks.items()):
        for t in held:
            block_copies.append(
                pltpu.make_async_remote_copy(
                    src_ref=mats[t].at[pl.ds(0, edge)],
                    dst_ref=block_in.at[i, t],
                    send_sem=block_send.at[i, t],
                    recv_sem=block_recv.at[i, t],
                    device_id=back(offset),
                    device_id_type=MESH,
                )
            )
    for copy in block_copies:
        copy.start()

    for load in loads[6:]:
        load.wait()
    slot_iota = lax.broadcasted_iota(jnp.int32, (slots, n_col), 0)
    weight = jnp.where(slot_iota < sink_count[...], sink_gain[...], 0.0)
    target = (sink_tile[...] * nodes + sink_node[...]).astype(F32)
    width = n_col * slots
    source = lax.broadcasted_iota(jnp.int32, (n_col, width), 0)
    place = lax.broadcasted_iota(jnp.int32, (n_col, width), 1)
    spread = jnp.where(place // slots == source, 1.0, 0.0)
    flat = dot(jnp.concatenate([target, weight], axis=0), spread)
    place = lax.broadcasted_iota(jnp.int32, (slots, width), 1)
    own = lax.rem(place, slots) == lax.broadcasted_iota(jnp.int32, (slots, width), 0)
    flat_target = jnp.sum(jnp.where(own, flat[:slots], 0.0), axis=0, keepdims=True)
    flat_weight = jnp.sum(jnp.where(own, flat[slots:], 0.0), axis=0, keepdims=True)
    node_row = lax.broadcasted_iota(jnp.int32, (2 * nodes, width), 0).astype(F32)
    scatter = jnp.where(node_row == flat_target, flat_weight, 0.0)

    base = [inject[t] - dot(conduct[t], volt[t]) for t in range(2)]

    def inside(offset):
        r, c = offset
        at_row, at_col = row + r, col + c
        return (at_row >= 0) & (at_row < n_row) & (at_col >= 0) & (at_col < n_col)

    present = {o: inside(o) for o in {**wide, **tracks}}

    def home(tile):
        return (tile[0], tile[1] // 2), tile[1] % 2

    def only_inside(tile, value):
        offset = home(tile)[0]
        return value if offset == (0, 0) else jnp.where(present[offset], value, 0.0)

    for copy in line_copies:
        copy.wait_recv()
    eye = lax.broadcasted_iota(jnp.int32, (edge, edge), 0) == lax.broadcasted_iota(
        jnp.int32, (edge, edge), 1
    )
    names = gain_lines(DEPTH - 1)
    place_of = {o: i for i, o in enumerate(tracks)}
    diagonals = []
    for way, tile in names:
        offset, t = home(tile)
        at = 2 * t + way
        if offset == (0, 0):
            line = track[at : at + 1, :]
        else:
            line = lines_in[place_of[offset], at : at + 1, 0:edge]
        diagonals.append(jnp.where(eye, only_inside(tile, line) * SCALE, 0.0))
    columns = dot(jnp.concatenate(diagonals, axis=0), jnp.ones((edge, nodes), F32))
    gains = {name: columns[i * edge : (i + 1) * edge] for i, name in enumerate(names)}

    def flow(tile, field):
        r, c = tile
        v = field[tile]
        total = gains[0, (r, c)] * (v - field[r, c + 1])
        total = total + gains[0, (r, c - 1)] * (v - field[r, c - 1])
        total = total + gains[1, (r, c)] * (v - field[r + 1, c])
        return total + gains[1, (r - 1, c)] * (v - field[r - 1, c])

    def gathered(depth, received, users, mine):
        field = {(0, t): mine[t] for t in range(2)}
        where = {o: i for i, o in enumerate(users)}
        for tile in near(depth):
            offset, t = home(tile)
            if offset != (0, 0):
                field[tile] = only_inside(tile, received[where[offset], t])
        return field

    own_tiles = ((0, 0), (0, 1))
    for copy in start_copies:
        copy.wait_recv()
    start = gathered(1, start_in, sides, [volt[t, 0:edge, :] for t in range(2)])
    first_flow = [flow(tile, start) for tile in own_tiles]
    calm = []
    for t in range(2):
        calm.append(
            jnp.concatenate(
                [base[t][:edge] - first_flow[t] * (1.0 / SCALE), base[t][edge:]], axis=0
            )
        )
    calm_rim = [dot(mats[t][0:edge, :], calm[t]) for t in range(2)]
    spread_rim = jnp.concatenate(
        [dot(mats[t][0:edge, :], scatter[t * nodes : (t + 1) * nodes]) for t in range(2)], axis=0
    )
    pltpu.make_async_copy(given.at[everything], given.at[everything], give_recv).wait()
    lift = dot(spread_rim, given[...])
    own_rim = [calm_rim[t] + lift[t * edge : (t + 1) * edge] for t in range(2)]
    for t in range(2):
        rims[t] = own_rim[t]
    rim_copies = copies(rims, rims_in, wide, rims_send, rims_recv)
    for copy in rim_copies:
        copy.start()
    current = dot(scatter, given[...])
    guess = []
    for t in range(2):
        resid = calm[t] + current[t * nodes : (t + 1) * nodes]
        rest = dot(mats[t][edge:, :], resid)
        guess.append(jnp.concatenate([own_rim[t], rest], axis=0))
        part = column_sum(guess[t], resid)
        moments = [part if t == 0 else moments[0] + part]
    for copy in block_copies:
        copy.wait_recv()
    block = {(0, t): mats[t][0:edge, 0:edge] for t in range(2)}
    block_at = {o: i for i, o in enumerate(blocks)}
    for tile in near(DEPTH - 1):
        offset, t = home(tile)
        if offset != (0, 0):
            block[tile] = block_in[block_at[offset], t, :, 0:edge]
    for copy in rim_copies:
        copy.wait_recv()

    field = gathered(DEPTH, rims_in, wide, own_rim)
    lifted, late_copies = [], []
    for step in range(3):
        reach = DEPTH - 1 - step
        if reach < 0:
            for t in range(2):
                late[t] = field[0, t]
            late_copies = copies(late, late_in, sides, late_send, late_recv)
            for copy in late_copies:
                copy.start()
            lifted.append([dot(mats[t][:, 0:edge], flows[0, t]) for t in range(2)])
            for copy in late_copies:
                copy.wait_recv()
            field = gathered(1, late_in, sides, [field[0, t] for t in range(2)])
            reach = 0
        flows = {tile: flow(tile, field) for tile in near(reach)}
        moments.append(sum(column_sum(field[0, t], flows[0, t]) for t in range(2)))
        if step < 2:
            if reach or DEPTH > 2:
                lifted.append([dot(mats[t][:, 0:edge], flows[0, t]) for t in range(2)])
            field = {
                tile: only_inside(tile, dot(block[tile], flows[tile])) for tile in near(reach)
            }
            moments.append(sum(column_sum(field[0, t], flows[0, t]) for t in range(2)))

    total = jnp.concatenate(moments + [jnp.zeros((2, nodes), F32)], axis=0)
    for r, (slot, group) in enumerate(((row, row_group), (col, col_group))):
        buf, count = (row_sums, col_sums)[r], len(group) + 1
        buf[slot] = total
        for peer in group:
            pltpu.make_async_remote_copy(
                src_ref=buf.at[slot],
                dst_ref=buf.at[slot],
                send_sem=sum_send.at[r],
                recv_sem=sum_recv.at[r],
                device_id=peer,
                device_id_type=MESH,
            ).start()
        part = buf.at[pl.ds(0, count - 1)]
        pltpu.make_async_copy(part, part, sum_recv.at[r]).wait()
        parts = [buf[i] for i in range(count)]
        while len(parts) > 1:
            pairs = [parts[i] + parts[i + 1] for i in range(0, len(parts) - 1, 2)]
            parts = pairs + ([parts[-1]] if len(parts) % 2 else [])
        total = parts[0]

    c0, c1, c2 = combination([total[i : i + 1] for i in range(6)])
    for t in range(2):
        out[t] = c0 * guess[t] + c1 * lifted[0][t] + c2 * lifted[1][t]

    for copy in line_copies + start_copies + block_copies + rim_copies + late_copies:
        copy.wait_send()
    pltpu.make_async_copy(ask.at[everything], ask.at[everything], ask_send).wait()
    pltpu.make_async_copy(give.at[everything], give.at[everything], give_send).wait()
    for r, group in enumerate((row_group, col_group)):
        part = (row_sums, col_sums)[r].at[pl.ds(0, len(group))]
        pltpu.make_async_copy(part, part, sum_send.at[r]).wait()


def local(
    initial_voltage,
    inject,
    conduct,
    capacitance,
    track_gain,
    driver_tile,
    sink_net,
    sink_count,
    sink_tile,
    sink_node,
    sink_gain,
):
    n_row, n_col = lax.axis_size("row"), lax.axis_size("col")
    tiles, nodes, patterns = initial_voltage.shape[1:]
    edge = track_gain.shape[-1]
    slots = sink_net.shape[-1]

    def by_slot(array):
        return jnp.swapaxes(array.reshape(n_col, slots), 0, 1)

    block = (tiles, nodes, patterns)
    arrays = (
        initial_voltage.reshape(block),
        inject.reshape(block),
        conduct.reshape(block),
        capacitance.reshape(tiles, nodes),
        track_gain.reshape(2 * tiles, edge),
        driver_tile.reshape(1, -1),
        by_slot(sink_net),
        sink_count.reshape(1, n_col),
        by_slot(sink_tile),
        by_slot(sink_node),
        by_slot(sink_gain),
    )
    rim = (tiles, edge, patterns)
    wide, blocks = from_devices(near(DEPTH)), from_devices(near(DEPTH - 1))
    tracks = from_devices([tile for _, tile in gain_lines(DEPTH - 1)])
    dma = pltpu.SemaphoreType.DMA
    slot_rows = pltpu.VMEM((n_col * slots, patterns), F32)
    result = pl.pallas_call(
        functools.partial(kernel, (n_row, n_col)),
        out_shape=pltpu.VMEM(block, F32),
        in_specs=[pl.BlockSpec(memory_space=pltpu.HBM)] * len(arrays),
        out_specs=pl.BlockSpec(memory_space=pltpu.VMEM),
        scratch_shapes=[
            *[pltpu.VMEM(array.shape, array.dtype) for array in arrays],
            pltpu.VMEM((nodes, nodes), F32),
            pltpu.VMEM((nodes, nodes), F32),
            *[slot_rows] * 4,
            pltpu.VMEM((8, patterns), F32),
            pltpu.VMEM((len(tracks), 8, patterns), F32),
            pltpu.VMEM((4, *rim), F32),
            pltpu.VMEM((len(blocks), *rim), F32),
            pltpu.VMEM(rim, F32),
            pltpu.VMEM((len(wide), *rim), F32),
            pltpu.VMEM(rim, F32),
            pltpu.VMEM((4, *rim), F32),
            pltpu.VMEM((n_row, 8, patterns), F32),
            pltpu.VMEM((n_col, 8, patterns), F32),
            dma((len(arrays),)),
            *[dma] * 4,
            *[dma((len(tracks),))] * 2,
            *[dma((4,))] * 2,
            *[dma((len(blocks), tiles))] * 2,
            *[dma((len(wide),))] * 2,
            *[dma((4,))] * 2,
            *[dma((2,))] * 2,
        ],
        compiler_params=pltpu.CompilerParams(
            collective_id=0, has_side_effects=True
        ),
        name="transient",
    )(*arrays)
    return initial_voltage + result.reshape(initial_voltage.shape)


def solution(mesh):
    four = P("row", "col", None, None)
    three = P("row", "col", None)
    placed = (four, four, four, three, four, three, four, three, four, four, four)
    return jax.shard_map(local, mesh=mesh, in_specs=placed, out_specs=four, check_vma=False)
```

```python
import functools

import jax
import jax.numpy as jnp
from jax import lax
from jax.experimental import pallas as pl
from jax.experimental.pallas import tpu as pltpu
from jax.sharding import PartitionSpec as P

F32 = jnp.float32
HIGH = lax.Precision.HIGHEST
MESH = pl.DeviceIdType.MESH
SCALE = 1.0 / 32.0
PIVOTS = 4
DEPTH = 3


def dot(left, right):
    return jnp.dot(left, right, precision=HIGH, preferred_element_type=F32)


def thirds(values):
    parts = []
    for _ in range(3):
        part = values.astype(jnp.bfloat16)
        parts.append(part)
        values = values - part.astype(F32)
    return parts


def dot_thirds(left, right):
    pairs = [(p, right) for p in left] if isinstance(left, list) else [(left, p) for p in right]
    first, second, third = (jnp.dot(a, b, preferred_element_type=F32) for a, b in pairs)
    return first + (second + third)


def lane_splat(block, lane):
    return jnp.take_along_axis(block, jnp.full(block.shape, lane, jnp.int32), axis=1)


def pivot_rows(rows, first, offset, lane):
    mine = [rows[offset + i : offset + i + 1] for i in range(PIVOTS)]
    splats = [lane_splat(rows, first + j) for j in range(PIVOTS)]
    small = [
        [splats[j][offset + i : offset + i + 1] for j in range(PIVOTS)]
        for i in range(PIVOTS)
    ]
    for j in range(PIVOTS):
        scale = 1.0 / small[j][j]
        row = [scale if m == j else small[j][m] * scale for m in range(PIVOTS)]
        for i in range(PIVOTS):
            if i == j:
                continue
            factor = small[i][j]
            small[i] = [
                -factor * scale if m == j else small[i][m] - factor * row[m]
                for m in range(PIVOTS)
            ]
        small[j] = row
    fresh = []
    for i in range(PIVOTS):
        total = small[i][0] * mine[0]
        for j in range(1, PIVOTS):
            total = total + small[i][j] * mine[j]
        for j in range(PIVOTS):
            total = jnp.where(lane == first + j, small[i][j], total)
        fresh.append(total)
    return fresh


def eliminate(mats, start, stop):
    nodes = mats[0].shape[0]
    lane = lax.broadcasted_iota(jnp.int32, (1, nodes), 1)

    def group(index, carry):
        base = pl.multiple_of(index * 8, 8)
        for offset in range(0, 8, PIVOTS):
            first = base + offset
            whole = [mat[...] for mat in mats]
            rows = [mat[pl.ds(base, 8), :] for mat in mats]
            fresh = [pivot_rows(r, first, offset, lane) for r in rows]
            kept = (lane >= first) & (lane < first + PIVOTS)
            done = []
            for t in range(len(mats)):
                total = jnp.where(kept, 0.0, whole[t])
                for j in range(PIVOTS):
                    total = total - lane_splat(whole[t], first + j) * fresh[t][j]
                done.append(total)
            for t, mat in enumerate(mats):
                mat[...] = done[t]
                for j in range(PIVOTS):
                    mat[pl.ds(first + j, 1), :] = fresh[t][j]
        return carry

    lax.fori_loop(start, stop, group, 0)


def ring_peers(position, high_count, low_count):
    high, low = position // low_count, lax.rem(position, low_count)
    offsets = [(a, b) for a in range(high_count) for b in range(low_count) if a or b]
    offsets.sort(key=lambda o: -(min(o[0], high_count - o[0]) + min(o[1], low_count - o[1])))
    return [
        lax.rem(high + a, high_count) * low_count + lax.rem(low + b, low_count)
        for a, b in offsets
    ]


def near(depth):
    span = range(-depth - 1, depth + 3)
    return [
        (r, c) for r in span for c in span if abs(r) + max(-c, 0, c - 1) <= depth
    ]


def from_devices(tiles):
    held = {}
    for r, c in tiles:
        held.setdefault((r, c // 2), []).append(c % 2)
    held.pop((0, 0), None)
    far = lambda o: -(2 * abs(o[1]) + abs(o[0]))
    return {o: sorted(held[o]) for o in sorted(held, key=far)}


def gain_lines(depth):
    east, south = [], []
    for r, c in near(depth):
        east += [(r, c), (r, c - 1)]
        south += [(r, c), (r - 1, c)]
    return [(0, t) for t in dict.fromkeys(east)] + [(1, t) for t in dict.fromkeys(south)]


def column_sum(left, right):
    return jnp.sum(left * right, axis=0, keepdims=True)


def safe_inverse(value):
    return jnp.where(value > 0.0, 1.0 / value, 0.0)


def combination(n):
    up = 1.0 / SCALE
    h00, h01, h02 = n[0] + up * n[1], n[1] + up * n[2], n[2] + up * n[3]
    h11, h12, h22 = h02, n[3] + up * n[4], n[4] + up * n[5]
    inv0 = safe_inverse(h00)
    l10, l20 = h01 * inv0, h02 * inv0
    d11, d12, d22 = h11 - l10 * h01, h12 - l10 * h02, h22 - l20 * h02
    g1, g2 = n[1] - l10 * n[0], n[2] - l20 * n[0]
    inv1 = safe_inverse(d11)
    l21 = d12 * inv1
    c2 = (g2 - l21 * g1) * safe_inverse(d22 - l21 * d12)
    c1 = (g1 - d12 * c2) * inv1
    c0 = (n[0] - h01 * c1 - h02 * c2) * inv0
    return c0, c1, c2


def kernel(
    sizes,
    volt_hbm,
    inject_hbm,
    conduct_hbm,
    cap_hbm,
    track_hbm,
    driver_tile_hbm,
    sink_net_hbm,
    sink_count_hbm,
    sink_tile_hbm,
    sink_node_hbm,
    sink_gain_hbm,
    out,
    volt,
    inject,
    conduct,
    cap,
    track,
    driver_tile,
    sink_net,
    sink_count,
    sink_tile,
    sink_node,
    sink_gain,
    mat0,
    mat1,
    ask,
    asked,
    give,
    given,
    lines,
    lines_in,
    start_in,
    block_in,
    rims,
    rims_in,
    late,
    late_in,
    row_sums,
    col_sums,
    load_sem,
    ask_send,
    ask_recv,
    give_send,
    give_recv,
    lines_send,
    lines_recv,
    start_send,
    start_recv,
    block_send,
    block_recv,
    rims_send,
    rims_recv,
    late_send,
    late_recv,
    sum_send,
    sum_recv,
):
    n_row, n_col = sizes
    row, col = lax.axis_index("row"), lax.axis_index("col")
    nodes, edge = volt.shape[1], track.shape[1]
    slots = sink_net.shape[0]
    nets = driver_tile.shape[1]

    row_group = [(position, col) for position in ring_peers(row, n_row // 2, 2)]
    col_group = [(row, position) for position in ring_peers(col, n_col // 4, 4)]
    wide = from_devices(near(DEPTH))
    blocks = from_devices(near(DEPTH - 1))
    tracks = from_devices([tile for _, tile in gain_lines(DEPTH - 1)])
    sides = from_devices(near(1))

    def device(offset):
        r, c = offset
        return (lax.rem(row + (n_row + r), n_row), lax.rem(col + (n_col + c), n_col))

    def back(offset):
        return device((-offset[0], -offset[1]))

    corners = [device(o) for o in wide if o[0] and o[1]]
    barrier = pltpu.get_barrier_semaphore()
    for peer in col_group + row_group + corners:
        pl.semaphore_signal(barrier, inc=1, device_id=peer, device_id_type=MESH)

    loads = [
        pltpu.make_async_copy(source, target, load_sem.at[i])
        for i, (source, target) in enumerate(
            (
                (sink_net_hbm, sink_net),
                (track_hbm, track),
                (volt_hbm, volt),
                (cap_hbm, cap),
                (conduct_hbm, conduct),
                (driver_tile_hbm, driver_tile),
                (sink_count_hbm, sink_count),
                (sink_tile_hbm, sink_tile),
                (sink_node_hbm, sink_node),
                (sink_gain_hbm, sink_gain),
                (inject_hbm, inject),
            )
        )
    ]
    for load in loads:
        load.start()

    loads[0].wait()
    wanted = sink_net[...].astype(F32)
    for s in range(n_col):
        ask[s * slots : (s + 1) * slots, :] = jnp.broadcast_to(
            wanted[:, s : s + 1], (slots, nodes)
        )
    loads[1].wait()
    lines[...] = jnp.zeros(lines.shape, F32)
    lines[0:4, 0:edge] = track[...]
    loads[2].wait()

    for load in loads[3:]:
        load.wait()
    slot_iota = lax.broadcasted_iota(jnp.int32, (slots, n_col), 0)
    weight = jnp.where(slot_iota < sink_count[...], sink_gain[...], 0.0)
    target = (sink_tile[...] * nodes + sink_node[...]).astype(F32)
    width = n_col * slots
    source = lax.broadcasted_iota(jnp.int32, (n_col, width), 0)
    place = lax.broadcasted_iota(jnp.int32, (n_col, width), 1)
    spread = jnp.where(place // slots == source, 1.0, 0.0)
    flat = dot(jnp.concatenate([target, weight], axis=0), spread)
    place = lax.broadcasted_iota(jnp.int32, (slots, width), 1)
    own = lax.rem(place, slots) == lax.broadcasted_iota(jnp.int32, (slots, width), 0)
    flat_target = jnp.sum(jnp.where(own, flat[:slots], 0.0), axis=0, keepdims=True)
    flat_weight = jnp.sum(jnp.where(own, flat[slots:], 0.0), axis=0, keepdims=True)
    node_row = lax.broadcasted_iota(jnp.int32, (2 * nodes, width), 0).astype(F32)
    scatter = jnp.where(node_row == flat_target, flat_weight, 0.0)

    base = [inject[t] - dot(conduct[t], volt[t]) for t in range(2)]

    lanes = lax.broadcasted_iota(jnp.int32, (1, 2 * nets), 1)
    tiles = jnp.concatenate([driver_tile[...], driver_tile[...]], axis=1)
    net_of = jnp.where(lanes >= nets, lanes - nets, lanes)
    tile_of = jnp.where(lanes >= nets, 1, 0)
    code = jnp.where(tiles == tile_of, net_of, -1).astype(F32)
    driver_rows = thirds(jnp.concatenate([volt[0, 0:nets, :], volt[1, 0:nets, :]], axis=0))


    pl.semaphore_wait(barrier, len(col_group) + len(row_group) + len(corners))

    def slot_rows(position):
        return pl.ds(pl.multiple_of(position * slots, slots), slots)

    def exchange(source, target, send, recv):
        for peer in col_group:
            pltpu.make_async_remote_copy(
                src_ref=source.at[slot_rows(peer[1])],
                dst_ref=target.at[slot_rows(col)],
                send_sem=send,
                recv_sem=recv,
                device_id=peer,
                device_id_type=MESH,
            ).start()

    def tile_part(ref, tiles):
        return ref if len(tiles) == 2 else ref.at[tiles[0]]

    def copies(sources, targets, users, send, recv):
        return [
            pltpu.make_async_remote_copy(
                src_ref=tile_part(sources, tiles),
                dst_ref=tile_part(targets.at[i], tiles),
                send_sem=send.at[i],
                recv_sem=recv.at[i],
                device_id=back(offset),
                device_id_type=MESH,
            )
            for i, (offset, tiles) in enumerate(users.items())
        ]

    exchange(ask, asked, ask_send, ask_recv)
    line_copies = [
        pltpu.make_async_remote_copy(
            src_ref=lines,
            dst_ref=lines_in.at[i],
            send_sem=lines_send.at[i],
            recv_sem=lines_recv.at[i],
            device_id=back(offset),
            device_id_type=MESH,
        )
        for i, offset in enumerate(tracks)
    ]
    start_copies = copies(volt.at[:, pl.ds(0, edge)], start_in, sides, start_send, start_recv)
    for copy in line_copies + start_copies:
        copy.start()
    asked[slot_rows(col), :] = ask[slot_rows(col), :]

    r_iota = lax.broadcasted_iota(jnp.int32, (nodes, nodes), 0)
    c_iota = lax.broadcasted_iota(jnp.int32, (nodes, nodes), 1)
    mats = (mat0, mat1)
    for t in range(2):
        mats[t][...] = conduct[t] + jnp.where(r_iota == c_iota, cap[t : t + 1, :], 0.0)
    groups = nodes // 8
    eliminate(mats, 0, groups // 2)

    everything = pl.ds(0, (n_col - 1) * slots)
    pltpu.make_async_copy(asked.at[everything], asked.at[everything], ask_recv).wait()
    pick = jnp.where(asked[...] == code, 1.0, 0.0).astype(jnp.bfloat16)
    give[...] = dot_thirds(pick, driver_rows)
    exchange(give, given, give_send, give_recv)
    given[slot_rows(col), :] = give[slot_rows(col), :]

    eliminate(mats, groups // 2, groups)
    block_copies = []
    for i, (offset, held) in enumerate(blocks.items()):
        for t in held:
            block_copies.append(
                pltpu.make_async_remote_copy(
                    src_ref=mats[t].at[pl.ds(0, edge)],
                    dst_ref=block_in.at[i, t],
                    send_sem=block_send.at[i, t],
                    recv_sem=block_recv.at[i, t],
                    device_id=back(offset),
                    device_id_type=MESH,
                )
            )
    for copy in block_copies:
        copy.start()

    def inside(offset):
        r, c = offset
        at_row, at_col = row + r, col + c
        return (at_row >= 0) & (at_row < n_row) & (at_col >= 0) & (at_col < n_col)

    present = {o: inside(o) for o in {**wide, **tracks}}

    def home(tile):
        return (tile[0], tile[1] // 2), tile[1] % 2

    def only_inside(tile, value):
        offset = home(tile)[0]
        return value if offset == (0, 0) else jnp.where(present[offset], value, 0.0)

    for copy in line_copies:
        copy.wait_recv()
    eye = lax.broadcasted_iota(jnp.int32, (edge, edge), 0) == lax.broadcasted_iota(
        jnp.int32, (edge, edge), 1
    )
    names = gain_lines(DEPTH - 1)
    place_of = {o: i for i, o in enumerate(tracks)}
    diagonals = []
    for way, tile in names:
        offset, t = home(tile)
        at = 2 * t + way
        if offset == (0, 0):
            line = track[at : at + 1, :]
        else:
            line = lines_in[place_of[offset], at : at + 1, 0:edge]
        diagonals.append(jnp.where(eye, only_inside(tile, line) * SCALE, 0.0))
    columns = dot_thirds(
        thirds(jnp.concatenate(diagonals, axis=0)), jnp.ones((edge, nodes), jnp.bfloat16)
    )
    gains = {name: columns[i * edge : (i + 1) * edge] for i, name in enumerate(names)}

    def flow(tile, field):
        r, c = tile
        v = field[tile]
        total = gains[0, (r, c)] * (v - field[r, c + 1])
        total = total + gains[0, (r, c - 1)] * (v - field[r, c - 1])
        total = total + gains[1, (r, c)] * (v - field[r + 1, c])
        return total + gains[1, (r - 1, c)] * (v - field[r - 1, c])

    def gathered(depth, received, users, mine):
        field = {(0, t): mine[t] for t in range(2)}
        where = {o: i for i, o in enumerate(users)}
        for tile in near(depth):
            offset, t = home(tile)
            if offset != (0, 0):
                field[tile] = only_inside(tile, received[where[offset], t])
        return field

    own_tiles = ((0, 0), (0, 1))
    for copy in start_copies:
        copy.wait_recv()
    start = gathered(1, start_in, sides, [volt[t, 0:edge, :] for t in range(2)])
    first_flow = [flow(tile, start) for tile in own_tiles]
    calm = []
    for t in range(2):
        calm.append(
            jnp.concatenate(
                [base[t][:edge] - first_flow[t] * (1.0 / SCALE), base[t][edge:]], axis=0
            )
        )
    calm_rim = [dot(mats[t][0:edge, :], calm[t]) for t in range(2)]
    spread_rim = jnp.concatenate(
        [dot(mats[t][0:edge, :], scatter[t * nodes : (t + 1) * nodes]) for t in range(2)], axis=0
    )
    pltpu.make_async_copy(given.at[everything], given.at[everything], give_recv).wait()
    lift = dot(spread_rim, given[...])
    own_rim = [calm_rim[t] + lift[t * edge : (t + 1) * edge] for t in range(2)]
    for t in range(2):
        rims[t] = own_rim[t]
    rim_copies = copies(rims, rims_in, wide, rims_send, rims_recv)
    for copy in rim_copies:
        copy.start()
    current = dot(scatter, given[...])
    guess = []
    for t in range(2):
        resid = calm[t] + current[t * nodes : (t + 1) * nodes]
        rest = dot(mats[t][edge:, :], resid)
        guess.append(jnp.concatenate([own_rim[t], rest], axis=0))
        part = column_sum(guess[t], resid)
        moments = [part if t == 0 else moments[0] + part]
    for copy in block_copies:
        copy.wait_recv()
    block = {(0, t): mats[t][0:edge, 0:edge] for t in range(2)}
    block_at = {o: i for i, o in enumerate(blocks)}
    for tile in near(DEPTH - 1):
        offset, t = home(tile)
        if offset != (0, 0):
            block[tile] = block_in[block_at[offset], t, :, 0:edge]
    for copy in rim_copies:
        copy.wait_recv()

    field = gathered(DEPTH, rims_in, wide, own_rim)
    lifted, late_copies = [], []
    for step in range(3):
        reach = DEPTH - 1 - step
        if reach < 0:
            for t in range(2):
                late[t] = field[0, t]
            late_copies = copies(late, late_in, sides, late_send, late_recv)
            for copy in late_copies:
                copy.start()
            lifted.append([dot(mats[t][:, 0:edge], flows[0, t]) for t in range(2)])
            for copy in late_copies:
                copy.wait_recv()
            field = gathered(1, late_in, sides, [field[0, t] for t in range(2)])
            reach = 0
        flows = {tile: flow(tile, field) for tile in near(reach)}
        moments.append(sum(column_sum(field[0, t], flows[0, t]) for t in range(2)))
        if step < 2:
            if reach or DEPTH > 2:
                lifted.append([dot(mats[t][:, 0:edge], flows[0, t]) for t in range(2)])
            field = {
                tile: only_inside(tile, dot(block[tile], flows[tile])) for tile in near(reach)
            }
            moments.append(sum(column_sum(field[0, t], flows[0, t]) for t in range(2)))

    total = jnp.concatenate(moments, axis=0)
    used = pl.ds(0, len(moments))
    for r, (slot, group) in enumerate(((row, row_group), (col, col_group))):
        buf, count = (row_sums, col_sums)[r], len(group) + 1
        buf[slot, used] = total
        for peer in group:
            pltpu.make_async_remote_copy(
                src_ref=buf.at[slot, used],
                dst_ref=buf.at[slot, used],
                send_sem=sum_send.at[r],
                recv_sem=sum_recv.at[r],
                device_id=peer,
                device_id_type=MESH,
            ).start()
        part = buf.at[pl.ds(0, count - 1), used]
        pltpu.make_async_copy(part, part, sum_recv.at[r]).wait()
        parts = [buf[i, used] for i in range(count)]
        while len(parts) > 1:
            pairs = [parts[i] + parts[i + 1] for i in range(0, len(parts) - 1, 2)]
            parts = pairs + ([parts[-1]] if len(parts) % 2 else [])
        total = parts[0]

    c0, c1, c2 = combination([total[i : i + 1] for i in range(6)])
    for t in range(2):
        out[t] = c0 * guess[t] + c1 * lifted[0][t] + c2 * lifted[1][t]

    for copy in line_copies + start_copies + block_copies + rim_copies + late_copies:
        copy.wait_send()
    pltpu.make_async_copy(ask.at[everything], ask.at[everything], ask_send).wait()
    pltpu.make_async_copy(give.at[everything], give.at[everything], give_send).wait()
    for r, group in enumerate((row_group, col_group)):
        part = (row_sums, col_sums)[r].at[pl.ds(0, len(group)), used]
        pltpu.make_async_copy(part, part, sum_send.at[r]).wait()


def local(
    initial_voltage,
    inject,
    conduct,
    capacitance,
    track_gain,
    driver_tile,
    sink_net,
    sink_count,
    sink_tile,
    sink_node,
    sink_gain,
):
    n_row, n_col = lax.axis_size("row"), lax.axis_size("col")
    tiles, nodes, patterns = initial_voltage.shape[1:]
    edge = track_gain.shape[-1]
    slots = sink_net.shape[-1]

    def by_slot(array):
        return jnp.swapaxes(array.reshape(n_col, slots), 0, 1)

    block = (tiles, nodes, patterns)
    arrays = (
        initial_voltage.reshape(block),
        inject.reshape(block),
        conduct.reshape(block),
        capacitance.reshape(tiles, nodes),
        track_gain.reshape(2 * tiles, edge),
        driver_tile.reshape(1, -1),
        by_slot(sink_net),
        sink_count.reshape(1, n_col),
        by_slot(sink_tile),
        by_slot(sink_node),
        by_slot(sink_gain),
    )
    rim = (tiles, edge, patterns)
    wide, blocks = from_devices(near(DEPTH)), from_devices(near(DEPTH - 1))
    tracks = from_devices([tile for _, tile in gain_lines(DEPTH - 1)])
    dma = pltpu.SemaphoreType.DMA
    slot_rows = pltpu.VMEM((n_col * slots, patterns), F32)
    result = pl.pallas_call(
        functools.partial(kernel, (n_row, n_col)),
        out_shape=pltpu.VMEM(block, F32),
        in_specs=[pl.BlockSpec(memory_space=pltpu.HBM)] * len(arrays),
        out_specs=pl.BlockSpec(memory_space=pltpu.VMEM),
        scratch_shapes=[
            *[pltpu.VMEM(array.shape, array.dtype) for array in arrays],
            pltpu.VMEM((nodes, nodes), F32),
            pltpu.VMEM((nodes, nodes), F32),
            *[slot_rows] * 4,
            pltpu.VMEM((8, patterns), F32),
            pltpu.VMEM((len(tracks), 8, patterns), F32),
            pltpu.VMEM((4, *rim), F32),
            pltpu.VMEM((len(blocks), *rim), F32),
            pltpu.VMEM(rim, F32),
            pltpu.VMEM((len(wide), *rim), F32),
            pltpu.VMEM(rim, F32),
            pltpu.VMEM((4, *rim), F32),
            pltpu.VMEM((n_row, 8, patterns), F32),
            pltpu.VMEM((n_col, 8, patterns), F32),
            dma((len(arrays),)),
            *[dma] * 4,
            *[dma((len(tracks),))] * 2,
            *[dma((4,))] * 2,
            *[dma((len(blocks), tiles))] * 2,
            *[dma((len(wide),))] * 2,
            *[dma((4,))] * 2,
            *[dma((2,))] * 2,
        ],
        compiler_params=pltpu.CompilerParams(
            collective_id=0, has_side_effects=True
        ),
        name="transient",
    )(*arrays)
    return initial_voltage + result.reshape(initial_voltage.shape)


def solution(mesh):
    four = P("row", "col", None, None)
    three = P("row", "col", None)
    placed = (four, four, four, three, four, three, four, three, four, four, four)
    return jax.shard_map(local, mesh=mesh, in_specs=placed, out_specs=four, check_vma=False)
```

```python
import functools

import jax
import jax.numpy as jnp
from jax import lax
from jax.experimental import pallas as pl
from jax.experimental.pallas import tpu as pltpu
from jax.sharding import PartitionSpec as P

F32 = jnp.float32
HIGH = lax.Precision.HIGHEST
MESH = pl.DeviceIdType.MESH
SCALE = 1.0 / 32.0
PIVOTS = 4
DEPTH = 3


def dot(left, right):
    return jnp.dot(left, right, precision=HIGH, preferred_element_type=F32)


def thirds(values):
    parts = []
    for _ in range(3):
        part = values.astype(jnp.bfloat16)
        parts.append(part)
        values = values - part.astype(F32)
    return parts


def dot_thirds(left, right):
    pairs = [(p, right) for p in left] if isinstance(left, list) else [(left, p) for p in right]
    first, second, third = (jnp.dot(a, b, preferred_element_type=F32) for a, b in pairs)
    return first + (second + third)


def lane_splat(block, lane):
    return jnp.take_along_axis(block, jnp.full(block.shape, lane, jnp.int32), axis=1)


def pivot_rows(rows, first, offset, lane):
    mine = [rows[offset + i : offset + i + 1] for i in range(PIVOTS)]
    splats = [lane_splat(rows, first + j) for j in range(PIVOTS)]
    small = [
        [splats[j][offset + i : offset + i + 1] for j in range(PIVOTS)]
        for i in range(PIVOTS)
    ]
    for j in range(PIVOTS):
        scale = 1.0 / small[j][j]
        row = [scale if m == j else small[j][m] * scale for m in range(PIVOTS)]
        for i in range(PIVOTS):
            if i == j:
                continue
            factor = small[i][j]
            small[i] = [
                -factor * scale if m == j else small[i][m] - factor * row[m]
                for m in range(PIVOTS)
            ]
        small[j] = row
    fresh = []
    for i in range(PIVOTS):
        total = small[i][0] * mine[0]
        for j in range(1, PIVOTS):
            total = total + small[i][j] * mine[j]
        for j in range(PIVOTS):
            total = jnp.where(lane == first + j, small[i][j], total)
        fresh.append(total)
    return fresh


def eliminate(mats, start, stop):
    nodes = mats[0].shape[0]
    lane = lax.broadcasted_iota(jnp.int32, (1, nodes), 1)

    def group(index, carry):
        base = pl.multiple_of(index * 8, 8)
        for offset in range(0, 8, PIVOTS):
            first = base + offset
            whole = [mat[...] for mat in mats]
            rows = [mat[pl.ds(base, 8), :] for mat in mats]
            fresh = [pivot_rows(r, first, offset, lane) for r in rows]
            kept = (lane >= first) & (lane < first + PIVOTS)
            done = []
            for t in range(len(mats)):
                total = jnp.where(kept, 0.0, whole[t])
                for j in range(PIVOTS):
                    total = total - lane_splat(whole[t], first + j) * fresh[t][j]
                done.append(total)
            for t, mat in enumerate(mats):
                mat[...] = done[t]
                for j in range(PIVOTS):
                    mat[pl.ds(first + j, 1), :] = fresh[t][j]
        return carry

    lax.fori_loop(start, stop, group, 0)


def ring_peers(position, high_count, low_count):
    high, low = position // low_count, lax.rem(position, low_count)
    offsets = [(a, b) for a in range(high_count) for b in range(low_count) if a or b]
    offsets.sort(key=lambda o: -(min(o[0], high_count - o[0]) + min(o[1], low_count - o[1])))
    return [
        lax.rem(high + a, high_count) * low_count + lax.rem(low + b, low_count)
        for a, b in offsets
    ]


def near(depth):
    span = range(-depth - 1, depth + 3)
    return [
        (r, c) for r in span for c in span if abs(r) + max(-c, 0, c - 1) <= depth
    ]


def from_devices(tiles):
    held = {}
    for r, c in tiles:
        held.setdefault((r, c // 2), []).append(c % 2)
    held.pop((0, 0), None)
    far = lambda o: -(2 * abs(o[1]) + abs(o[0]))
    return {o: sorted(held[o]) for o in sorted(held, key=far)}


def gain_lines(depth):
    east, south = [], []
    for r, c in near(depth):
        east += [(r, c), (r, c - 1)]
        south += [(r, c), (r - 1, c)]
    return [(0, t) for t in dict.fromkeys(east)] + [(1, t) for t in dict.fromkeys(south)]


def column_sum(left, right):
    return jnp.sum(left * right, axis=0, keepdims=True)


def safe_inverse(value):
    return jnp.where(value > 0.0, 1.0 / value, 0.0)


def combination(n):
    up = 1.0 / SCALE
    h00, h01, h02 = n[0] + up * n[1], n[1] + up * n[2], n[2] + up * n[3]
    h11, h12, h22 = h02, n[3] + up * n[4], n[4] + up * n[5]
    inv0 = safe_inverse(h00)
    l10, l20 = h01 * inv0, h02 * inv0
    d11, d12, d22 = h11 - l10 * h01, h12 - l10 * h02, h22 - l20 * h02
    g1, g2 = n[1] - l10 * n[0], n[2] - l20 * n[0]
    inv1 = safe_inverse(d11)
    l21 = d12 * inv1
    c2 = (g2 - l21 * g1) * safe_inverse(d22 - l21 * d12)
    c1 = (g1 - d12 * c2) * inv1
    c0 = (n[0] - h01 * c1 - h02 * c2) * inv0
    return c0, c1, c2


def kernel(
    sizes,
    volt_hbm,
    inject_hbm,
    conduct_hbm,
    cap_hbm,
    track_hbm,
    driver_tile_hbm,
    sink_net_hbm,
    sink_count_hbm,
    sink_tile_hbm,
    sink_node_hbm,
    sink_gain_hbm,
    out,
    volt,
    inject,
    conduct,
    cap,
    track,
    driver_tile,
    sink_net,
    sink_count,
    sink_tile,
    sink_node,
    sink_gain,
    mat0,
    mat1,
    ask,
    asked,
    give,
    given,
    lines,
    lines_in,
    start_in,
    block_in,
    rims,
    rims_in,
    late,
    late_in,
    row_sums,
    col_sums,
    load_sem,
    ask_send,
    ask_recv,
    give_send,
    give_recv,
    lines_send,
    lines_recv,
    start_send,
    start_recv,
    block_send,
    block_recv,
    rims_send,
    rims_recv,
    late_send,
    late_recv,
    sum_send,
    sum_recv,
):
    n_row, n_col = sizes
    row, col = lax.axis_index("row"), lax.axis_index("col")
    nodes, edge = volt.shape[1], track.shape[1]
    slots = sink_net.shape[0]
    nets = driver_tile.shape[1]

    row_group = [(position, col) for position in ring_peers(row, n_row // 2, 2)]
    col_group = [(row, position) for position in ring_peers(col, n_col // 4, 4)]
    wide = from_devices(near(DEPTH))
    blocks = from_devices(near(DEPTH - 1))
    tracks = from_devices([tile for _, tile in gain_lines(DEPTH - 1)])
    sides = from_devices(near(1))

    def device(offset):
        r, c = offset
        return (lax.rem(row + (n_row + r), n_row), lax.rem(col + (n_col + c), n_col))

    def back(offset):
        return device((-offset[0], -offset[1]))

    corners = [device(o) for o in wide if o[0] and o[1]]
    barrier = pltpu.get_barrier_semaphore()
    for peer in col_group + row_group + corners:
        pl.semaphore_signal(barrier, inc=1, device_id=peer, device_id_type=MESH)

    loads = [
        pltpu.make_async_copy(source, target, load_sem.at[i])
        for i, (source, target) in enumerate(
            (
                (sink_net_hbm, sink_net),
                (track_hbm, track),
                (volt_hbm, volt),
                (cap_hbm, cap),
                (conduct_hbm, conduct),
                (driver_tile_hbm, driver_tile),
                (sink_count_hbm, sink_count),
                (sink_tile_hbm, sink_tile),
                (sink_node_hbm, sink_node),
                (sink_gain_hbm, sink_gain),
                (inject_hbm, inject),
            )
        )
    ]
    for load in loads:
        load.start()

    loads[0].wait()
    wanted = sink_net[...].astype(jnp.bfloat16)
    to_lane = jnp.where(
        lax.broadcasted_iota(jnp.int32, (slots, nodes), 0)
        == lax.broadcasted_iota(jnp.int32, (slots, nodes), 1),
        1.0,
        0.0,
    ).astype(jnp.bfloat16)
    ask[pl.ds(0, n_col, stride=slots), :] = lax.dot_general(
        wanted, to_lane, (((0,), (0,)), ((), ())), preferred_element_type=F32
    )
    loads[1].wait()
    lines[...] = jnp.zeros(lines.shape, F32)
    lines[0:4, 0:edge] = track[...]
    loads[2].wait()

    for load in loads[3:]:
        load.wait()
    slot_iota = lax.broadcasted_iota(jnp.int32, (slots, n_col), 0)
    weight = jnp.where(slot_iota < sink_count[...], sink_gain[...], 0.0)
    target = (sink_tile[...] * nodes + sink_node[...]).astype(F32)
    width = n_col * slots
    source = lax.broadcasted_iota(jnp.int32, (n_col, width), 0)
    place = lax.broadcasted_iota(jnp.int32, (n_col, width), 1)
    spread = jnp.where(place // slots == source, 1.0, 0.0)
    flat = dot(jnp.concatenate([target, weight], axis=0), spread)
    place = lax.broadcasted_iota(jnp.int32, (slots, width), 1)
    own = lax.rem(place, slots) == lax.broadcasted_iota(jnp.int32, (slots, width), 0)
    flat_target = jnp.sum(jnp.where(own, flat[:slots], 0.0), axis=0, keepdims=True)
    flat_weight = jnp.sum(jnp.where(own, flat[slots:], 0.0), axis=0, keepdims=True)
    node_row = lax.broadcasted_iota(jnp.int32, (2 * nodes, width), 0).astype(F32)
    scatter = jnp.where(node_row == flat_target, flat_weight, 0.0)

    base = [inject[t] - dot(conduct[t], volt[t]) for t in range(2)]

    lanes = lax.broadcasted_iota(jnp.int32, (1, 2 * nets), 1)
    tiles = jnp.concatenate([driver_tile[...], driver_tile[...]], axis=1)
    net_of = jnp.where(lanes >= nets, lanes - nets, lanes)
    tile_of = jnp.where(lanes >= nets, 1, 0)
    code = jnp.where(tiles == tile_of, net_of, -1).astype(F32)
    driver_rows = thirds(jnp.concatenate([volt[0, 0:nets, :], volt[1, 0:nets, :]], axis=0))


    pl.semaphore_wait(barrier, len(col_group) + len(row_group) + len(corners))

    def slot_rows(position, count=slots):
        return pl.ds(pl.multiple_of(position * slots, slots), count)

    def exchange(source, target, send, recv, count=slots):
        for peer in col_group:
            pltpu.make_async_remote_copy(
                src_ref=source.at[slot_rows(peer[1], count)],
                dst_ref=target.at[slot_rows(col, count)],
                send_sem=send,
                recv_sem=recv,
                device_id=peer,
                device_id_type=MESH,
            ).start()

    def tile_part(ref, tiles):
        return ref if len(tiles) == 2 else ref.at[tiles[0]]

    def copies(sources, targets, users, send, recv):
        return [
            pltpu.make_async_remote_copy(
                src_ref=tile_part(sources, tiles),
                dst_ref=tile_part(targets.at[i], tiles),
                send_sem=send.at[i],
                recv_sem=recv.at[i],
                device_id=back(offset),
                device_id_type=MESH,
            )
            for i, (offset, tiles) in enumerate(users.items())
        ]

    exchange(ask, asked, ask_send, ask_recv, 1)
    line_copies = [
        pltpu.make_async_remote_copy(
            src_ref=lines,
            dst_ref=lines_in.at[i],
            send_sem=lines_send.at[i],
            recv_sem=lines_recv.at[i],
            device_id=back(offset),
            device_id_type=MESH,
        )
        for i, offset in enumerate(tracks)
    ]
    start_copies = copies(volt.at[:, pl.ds(0, edge)], start_in, sides, start_send, start_recv)
    for copy in line_copies + start_copies:
        copy.start()
    asked[slot_rows(col, 1), :] = ask[slot_rows(col, 1), :]

    r_iota = lax.broadcasted_iota(jnp.int32, (nodes, nodes), 0)
    c_iota = lax.broadcasted_iota(jnp.int32, (nodes, nodes), 1)
    mats = (mat0, mat1)
    for t in range(2):
        mats[t][...] = conduct[t] + jnp.where(r_iota == c_iota, cap[t : t + 1, :], 0.0)
    groups = nodes // 8
    eliminate(mats, 0, groups // 2)

    everything, each = pl.ds(0, (n_col - 1) * slots), pl.ds(0, n_col - 1)
    pltpu.make_async_copy(asked.at[each], asked.at[each], ask_recv).wait()
    wish = asked[pl.ds(0, n_col, stride=slots), :]
    pick = jnp.concatenate(
        [
            jnp.where(jnp.broadcast_to(wish[:, k : k + 1], (n_col, 2 * nets)) == code, 1.0, 0.0)
            for k in range(slots)
        ],
        axis=0,
    ).astype(jnp.bfloat16)
    answer = dot_thirds(pick, driver_rows)
    for k in range(slots):
        give[pl.ds(k, n_col, stride=slots), :] = answer[k * n_col : (k + 1) * n_col]
    exchange(give, given, give_send, give_recv)
    given[slot_rows(col), :] = give[slot_rows(col), :]

    eliminate(mats, groups // 2, groups)
    block_copies = []
    for i, (offset, held) in enumerate(blocks.items()):
        for t in held:
            block_copies.append(
                pltpu.make_async_remote_copy(
                    src_ref=mats[t].at[pl.ds(0, edge)],
                    dst_ref=block_in.at[i, t],
                    send_sem=block_send.at[i, t],
                    recv_sem=block_recv.at[i, t],
                    device_id=back(offset),
                    device_id_type=MESH,
                )
            )
    for copy in block_copies:
        copy.start()

    def inside(offset):
        r, c = offset
        at_row, at_col = row + r, col + c
        return (at_row >= 0) & (at_row < n_row) & (at_col >= 0) & (at_col < n_col)

    present = {o: inside(o) for o in {**wide, **tracks}}

    def home(tile):
        return (tile[0], tile[1] // 2), tile[1] % 2

    def only_inside(tile, value):
        offset = home(tile)[0]
        return value if offset == (0, 0) else jnp.where(present[offset], value, 0.0)

    for copy in line_copies:
        copy.wait_recv()
    eye = lax.broadcasted_iota(jnp.int32, (edge, edge), 0) == lax.broadcasted_iota(
        jnp.int32, (edge, edge), 1
    )
    names = gain_lines(DEPTH - 1)
    place_of = {o: i for i, o in enumerate(tracks)}
    diagonals = []
    for way, tile in names:
        offset, t = home(tile)
        at = 2 * t + way
        if offset == (0, 0):
            line = track[at : at + 1, :]
        else:
            line = lines_in[place_of[offset], at : at + 1, 0:edge]
        diagonals.append(jnp.where(eye, only_inside(tile, line) * SCALE, 0.0))
    columns = dot_thirds(
        thirds(jnp.concatenate(diagonals, axis=0)), jnp.ones((edge, nodes), jnp.bfloat16)
    )
    gains = {name: columns[i * edge : (i + 1) * edge] for i, name in enumerate(names)}

    def flow(tile, field):
        r, c = tile
        v = field[tile]
        total = gains[0, (r, c)] * (v - field[r, c + 1])
        total = total + gains[0, (r, c - 1)] * (v - field[r, c - 1])
        total = total + gains[1, (r, c)] * (v - field[r + 1, c])
        return total + gains[1, (r - 1, c)] * (v - field[r - 1, c])

    def gathered(depth, received, users, mine):
        field = {(0, t): mine[t] for t in range(2)}
        where = {o: i for i, o in enumerate(users)}
        for tile in near(depth):
            offset, t = home(tile)
            if offset != (0, 0):
                field[tile] = only_inside(tile, received[where[offset], t])
        return field

    own_tiles = ((0, 0), (0, 1))
    for copy in start_copies:
        copy.wait_recv()
    start = gathered(1, start_in, sides, [volt[t, 0:edge, :] for t in range(2)])
    first_flow = [flow(tile, start) for tile in own_tiles]
    calm = []
    for t in range(2):
        calm.append(
            jnp.concatenate(
                [base[t][:edge] - first_flow[t] * (1.0 / SCALE), base[t][edge:]], axis=0
            )
        )
    calm_rim = [dot(mats[t][0:edge, :], calm[t]) for t in range(2)]
    spread_rim = jnp.concatenate(
        [dot(mats[t][0:edge, :], scatter[t * nodes : (t + 1) * nodes]) for t in range(2)], axis=0
    )
    pltpu.make_async_copy(given.at[everything], given.at[everything], give_recv).wait()
    lift = dot(spread_rim, given[...])
    own_rim = [calm_rim[t] + lift[t * edge : (t + 1) * edge] for t in range(2)]
    for t in range(2):
        rims[t] = own_rim[t]
    rim_copies = copies(rims, rims_in, wide, rims_send, rims_recv)
    for copy in rim_copies:
        copy.start()
    current = dot(scatter, given[...])
    guess = []
    for t in range(2):
        resid = calm[t] + current[t * nodes : (t + 1) * nodes]
        rest = dot(mats[t][edge:, :], resid)
        guess.append(jnp.concatenate([own_rim[t], rest], axis=0))
        part = column_sum(guess[t], resid)
        moments = [part if t == 0 else moments[0] + part]
    for copy in block_copies:
        copy.wait_recv()
    block = {(0, t): mats[t][0:edge, 0:edge] for t in range(2)}
    block_at = {o: i for i, o in enumerate(blocks)}
    for tile in near(DEPTH - 1):
        offset, t = home(tile)
        if offset != (0, 0):
            block[tile] = block_in[block_at[offset], t, :, 0:edge]
    for copy in rim_copies:
        copy.wait_recv()

    field = gathered(DEPTH, rims_in, wide, own_rim)
    lifted, late_copies = [], []
    for step in range(3):
        reach = DEPTH - 1 - step
        if reach < 0:
            for t in range(2):
                late[t] = field[0, t]
            late_copies = copies(late, late_in, sides, late_send, late_recv)
            for copy in late_copies:
                copy.start()
            lifted.append([dot(mats[t][:, 0:edge], flows[0, t]) for t in range(2)])
            for copy in late_copies:
                copy.wait_recv()
            field = gathered(1, late_in, sides, [field[0, t] for t in range(2)])
            reach = 0
        flows = {tile: flow(tile, field) for tile in near(reach)}
        moments.append(sum(column_sum(field[0, t], flows[0, t]) for t in range(2)))
        if step < 2:
            if reach or DEPTH > 2:
                lifted.append([dot(mats[t][:, 0:edge], flows[0, t]) for t in range(2)])
            field = {
                tile: only_inside(tile, dot(block[tile], flows[tile])) for tile in near(reach)
            }
            moments.append(sum(column_sum(field[0, t], flows[0, t]) for t in range(2)))

    total = jnp.concatenate(moments, axis=0)
    used = pl.ds(0, len(moments))
    for r, (slot, group) in enumerate(((row, row_group), (col, col_group))):
        buf, count = (row_sums, col_sums)[r], len(group) + 1
        buf[slot, used] = total
        for peer in group:
            pltpu.make_async_remote_copy(
                src_ref=buf.at[slot, used],
                dst_ref=buf.at[slot, used],
                send_sem=sum_send.at[r],
                recv_sem=sum_recv.at[r],
                device_id=peer,
                device_id_type=MESH,
            ).start()
        part = buf.at[pl.ds(0, count - 1), used]
        pltpu.make_async_copy(part, part, sum_recv.at[r]).wait()
        parts = [buf[i, used] for i in range(count)]
        while len(parts) > 1:
            pairs = [parts[i] + parts[i + 1] for i in range(0, len(parts) - 1, 2)]
            parts = pairs + ([parts[-1]] if len(parts) % 2 else [])
        total = parts[0]

    c0, c1, c2 = combination([total[i : i + 1] for i in range(6)])
    for t in range(2):
        out[t] = c0 * guess[t] + c1 * lifted[0][t] + c2 * lifted[1][t]

    for copy in line_copies + start_copies + block_copies + rim_copies + late_copies:
        copy.wait_send()
    pltpu.make_async_copy(ask.at[each], ask.at[each], ask_send).wait()
    pltpu.make_async_copy(give.at[everything], give.at[everything], give_send).wait()
    for r, group in enumerate((row_group, col_group)):
        part = (row_sums, col_sums)[r].at[pl.ds(0, len(group)), used]
        pltpu.make_async_copy(part, part, sum_send.at[r]).wait()


def local(
    initial_voltage,
    inject,
    conduct,
    capacitance,
    track_gain,
    driver_tile,
    sink_net,
    sink_count,
    sink_tile,
    sink_node,
    sink_gain,
):
    n_row, n_col = lax.axis_size("row"), lax.axis_size("col")
    tiles, nodes, patterns = initial_voltage.shape[1:]
    edge = track_gain.shape[-1]
    slots = sink_net.shape[-1]

    def by_slot(array):
        return jnp.swapaxes(array.reshape(n_col, slots), 0, 1)

    block = (tiles, nodes, patterns)
    arrays = (
        initial_voltage.reshape(block),
        inject.reshape(block),
        conduct.reshape(block),
        capacitance.reshape(tiles, nodes),
        track_gain.reshape(2 * tiles, edge),
        driver_tile.reshape(1, -1),
        by_slot(sink_net),
        sink_count.reshape(1, n_col),
        by_slot(sink_tile),
        by_slot(sink_node),
        by_slot(sink_gain),
    )
    rim = (tiles, edge, patterns)
    wide, blocks = from_devices(near(DEPTH)), from_devices(near(DEPTH - 1))
    tracks = from_devices([tile for _, tile in gain_lines(DEPTH - 1)])
    dma = pltpu.SemaphoreType.DMA
    slot_rows = pltpu.VMEM((n_col * slots, patterns), F32)
    result = pl.pallas_call(
        functools.partial(kernel, (n_row, n_col)),
        out_shape=pltpu.VMEM(block, F32),
        in_specs=[pl.BlockSpec(memory_space=pltpu.HBM)] * len(arrays),
        out_specs=pl.BlockSpec(memory_space=pltpu.VMEM),
        scratch_shapes=[
            *[pltpu.VMEM(array.shape, array.dtype) for array in arrays],
            pltpu.VMEM((nodes, nodes), F32),
            pltpu.VMEM((nodes, nodes), F32),
            *[slot_rows] * 4,
            pltpu.VMEM((8, patterns), F32),
            pltpu.VMEM((len(tracks), 8, patterns), F32),
            pltpu.VMEM((4, *rim), F32),
            pltpu.VMEM((len(blocks), *rim), F32),
            pltpu.VMEM(rim, F32),
            pltpu.VMEM((len(wide), *rim), F32),
            pltpu.VMEM(rim, F32),
            pltpu.VMEM((4, *rim), F32),
            pltpu.VMEM((n_row, 8, patterns), F32),
            pltpu.VMEM((n_col, 8, patterns), F32),
            dma((len(arrays),)),
            *[dma] * 4,
            *[dma((len(tracks),))] * 2,
            *[dma((4,))] * 2,
            *[dma((len(blocks), tiles))] * 2,
            *[dma((len(wide),))] * 2,
            *[dma((4,))] * 2,
            *[dma((2,))] * 2,
        ],
        compiler_params=pltpu.CompilerParams(
            collective_id=0, has_side_effects=True
        ),
        name="transient",
    )(*arrays)
    return initial_voltage + result.reshape(initial_voltage.shape)


def solution(mesh):
    four = P("row", "col", None, None)
    three = P("row", "col", None)
    placed = (four, four, four, three, four, three, four, three, four, four, four)
    return jax.shard_map(local, mesh=mesh, in_specs=placed, out_specs=four, check_vma=False)
```

```python
import functools

import jax
import jax.numpy as jnp
from jax import lax
from jax.experimental import pallas as pl
from jax.experimental.pallas import tpu as pltpu
from jax.sharding import PartitionSpec as P

F32 = jnp.float32
HIGH = lax.Precision.HIGHEST
MESH = pl.DeviceIdType.MESH
SCALE = 1.0 / 32.0
PIVOTS = 4
DEPTH = 3


def dot(left, right):
    return jnp.dot(left, right, precision=HIGH, preferred_element_type=F32)


def thirds(values):
    parts = []
    for _ in range(3):
        part = values.astype(jnp.bfloat16)
        parts.append(part)
        values = values - part.astype(F32)
    return parts


def dot_thirds(left, right):
    pairs = [(p, right) for p in left] if isinstance(left, list) else [(left, p) for p in right]
    first, second, third = (jnp.dot(a, b, preferred_element_type=F32) for a, b in pairs)
    return first + (second + third)


def lane_splat(block, lane):
    return jnp.take_along_axis(block, jnp.full(block.shape, lane, jnp.int32), axis=1)


def pivot_rows(rows, first, offset, lane):
    mine = [rows[offset + i : offset + i + 1] for i in range(PIVOTS)]
    splats = [lane_splat(rows, first + j) for j in range(PIVOTS)]
    small = [
        [splats[j][offset + i : offset + i + 1] for j in range(PIVOTS)]
        for i in range(PIVOTS)
    ]
    for j in range(PIVOTS):
        scale = 1.0 / small[j][j]
        row = [scale if m == j else small[j][m] * scale for m in range(PIVOTS)]
        for i in range(PIVOTS):
            if i == j:
                continue
            factor = small[i][j]
            small[i] = [
                -factor * scale if m == j else small[i][m] - factor * row[m]
                for m in range(PIVOTS)
            ]
        small[j] = row
    fresh = []
    for i in range(PIVOTS):
        total = small[i][0] * mine[0]
        for j in range(1, PIVOTS):
            total = total + small[i][j] * mine[j]
        for j in range(PIVOTS):
            total = jnp.where(lane == first + j, small[i][j], total)
        fresh.append(total)
    return fresh


def eliminate(mats, start, stop):
    nodes = mats[0].shape[0]
    lane = lax.broadcasted_iota(jnp.int32, (1, nodes), 1)

    def group(index, carry):
        base = pl.multiple_of(index * 8, 8)
        for offset in range(0, 8, PIVOTS):
            first = base + offset
            whole = [mat[...] for mat in mats]
            rows = [mat[pl.ds(base, 8), :] for mat in mats]
            fresh = [pivot_rows(r, first, offset, lane) for r in rows]
            kept = (lane >= first) & (lane < first + PIVOTS)
            done = []
            for t in range(len(mats)):
                total = jnp.where(kept, 0.0, whole[t])
                for j in range(PIVOTS):
                    total = total - lane_splat(whole[t], first + j) * fresh[t][j]
                done.append(total)
            for t, mat in enumerate(mats):
                mat[...] = done[t]
                for j in range(PIVOTS):
                    mat[pl.ds(first + j, 1), :] = fresh[t][j]
        return carry

    lax.fori_loop(start, stop, group, 0)


def ring_peers(position, high_count, low_count):
    high, low = position // low_count, lax.rem(position, low_count)
    offsets = [(a, b) for a in range(high_count) for b in range(low_count) if a or b]
    offsets.sort(key=lambda o: -(min(o[0], high_count - o[0]) + min(o[1], low_count - o[1])))
    return [
        lax.rem(high + a, high_count) * low_count + lax.rem(low + b, low_count)
        for a, b in offsets
    ]


def near(depth):
    span = range(-depth - 1, depth + 3)
    return [
        (r, c) for r in span for c in span if abs(r) + max(-c, 0, c - 1) <= depth
    ]


def from_devices(tiles):
    held = {}
    for r, c in tiles:
        held.setdefault((r, c // 2), []).append(c % 2)
    held.pop((0, 0), None)
    far = lambda o: -(2 * abs(o[1]) + abs(o[0]))
    return {o: sorted(held[o]) for o in sorted(held, key=far)}


def gain_lines(depth):
    east, south = [], []
    for r, c in near(depth):
        east += [(r, c), (r, c - 1)]
        south += [(r, c), (r - 1, c)]
    return [(0, t) for t in dict.fromkeys(east)] + [(1, t) for t in dict.fromkeys(south)]


def column_sum(left, right):
    return jnp.sum(left * right, axis=0, keepdims=True)


def safe_inverse(value):
    return jnp.where(value > 0.0, 1.0 / value, 0.0)


def combination(n):
    up = 1.0 / SCALE
    h00, h01, h02 = n[0] + up * n[1], n[1] + up * n[2], n[2] + up * n[3]
    h11, h12, h22 = h02, n[3] + up * n[4], n[4] + up * n[5]
    inv0 = safe_inverse(h00)
    l10, l20 = h01 * inv0, h02 * inv0
    d11, d12, d22 = h11 - l10 * h01, h12 - l10 * h02, h22 - l20 * h02
    g1, g2 = n[1] - l10 * n[0], n[2] - l20 * n[0]
    inv1 = safe_inverse(d11)
    l21 = d12 * inv1
    c2 = (g2 - l21 * g1) * safe_inverse(d22 - l21 * d12)
    c1 = (g1 - d12 * c2) * inv1
    c0 = (n[0] - h01 * c1 - h02 * c2) * inv0
    return c0, c1, c2


def kernel(
    sizes,
    volt_hbm,
    inject_hbm,
    conduct_hbm,
    cap_hbm,
    track_hbm,
    driver_tile_hbm,
    sink_net_hbm,
    sink_count_hbm,
    sink_tile_hbm,
    sink_node_hbm,
    sink_gain_hbm,
    out,
    volt,
    inject,
    conduct,
    cap,
    track,
    driver_tile,
    sink_net,
    sink_count,
    sink_tile,
    sink_node,
    sink_gain,
    mat0,
    mat1,
    ask,
    asked,
    give,
    given,
    lines,
    lines_in,
    start_in,
    block_in,
    rims,
    rims_in,
    late,
    late_in,
    row_sums,
    col_sums,
    load_sem,
    ask_send,
    ask_recv,
    give_send,
    give_recv,
    lines_send,
    lines_recv,
    start_send,
    start_recv,
    block_send,
    block_recv,
    rims_send,
    rims_recv,
    late_send,
    late_recv,
    sum_send,
    sum_recv,
):
    n_row, n_col = sizes
    row, col = lax.axis_index("row"), lax.axis_index("col")
    nodes, edge = volt.shape[1], track.shape[1]
    slots = sink_net.shape[0]
    nets = driver_tile.shape[1]

    row_group = [(position, col) for position in ring_peers(row, n_row // 2, 2)]
    col_group = [(row, position) for position in ring_peers(col, n_col // 4, 4)]
    wide = from_devices(near(DEPTH))
    blocks = from_devices(near(DEPTH - 1))
    tracks = from_devices([tile for _, tile in gain_lines(DEPTH - 1)])
    sides = from_devices(near(1))

    def device(offset):
        r, c = offset
        return (lax.rem(row + (n_row + r), n_row), lax.rem(col + (n_col + c), n_col))

    def back(offset):
        return device((-offset[0], -offset[1]))

    corners = [device(o) for o in wide if o[0] and o[1]]
    barrier = pltpu.get_barrier_semaphore()
    for peer in col_group + row_group + corners:
        pl.semaphore_signal(barrier, inc=1, device_id=peer, device_id_type=MESH)

    loads = [
        pltpu.make_async_copy(source, target, load_sem.at[i])
        for i, (source, target) in enumerate(
            (
                (sink_net_hbm, sink_net),
                (track_hbm, track),
                (volt_hbm, volt),
                (cap_hbm, cap),
                (conduct_hbm, conduct),
                (driver_tile_hbm, driver_tile),
                (sink_count_hbm, sink_count),
                (sink_tile_hbm, sink_tile),
                (sink_node_hbm, sink_node),
                (sink_gain_hbm, sink_gain),
                (inject_hbm, inject),
            )
        )
    ]
    for load in loads:
        load.start()

    loads[0].wait()
    wanted = sink_net[...].astype(jnp.bfloat16)
    to_lane = jnp.where(
        lax.broadcasted_iota(jnp.int32, (slots, nodes), 0)
        == lax.broadcasted_iota(jnp.int32, (slots, nodes), 1),
        1.0,
        0.0,
    ).astype(jnp.bfloat16)
    ask[pl.ds(0, n_col, stride=slots), :] = lax.dot_general(
        wanted, to_lane, (((0,), (0,)), ((), ())), preferred_element_type=F32
    )
    loads[1].wait()
    lines[...] = jnp.zeros(lines.shape, F32)
    lines[0:4, 0:edge] = track[...]
    loads[2].wait()

    for load in loads[3:]:
        load.wait()
    slot_iota = lax.broadcasted_iota(jnp.int32, (slots, n_col), 0)
    weight = jnp.where(slot_iota < sink_count[...], sink_gain[...], 0.0)
    target = (sink_tile[...] * nodes + sink_node[...]).astype(F32)
    width = n_col * slots
    source = lax.broadcasted_iota(jnp.int32, (n_col, width), 0)
    place = lax.broadcasted_iota(jnp.int32, (n_col, width), 1)
    spread = jnp.where(place // slots == source, 1.0, 0.0)
    flat = dot(jnp.concatenate([target, weight], axis=0), spread)
    place = lax.broadcasted_iota(jnp.int32, (slots, width), 1)
    own = lax.rem(place, slots) == lax.broadcasted_iota(jnp.int32, (slots, width), 0)
    flat_target = jnp.sum(jnp.where(own, flat[:slots], 0.0), axis=0, keepdims=True)
    flat_weight = jnp.sum(jnp.where(own, flat[slots:], 0.0), axis=0, keepdims=True)
    node_row = lax.broadcasted_iota(jnp.int32, (2 * nodes, width), 0).astype(F32)
    scatter = jnp.where(node_row == flat_target, flat_weight, 0.0)

    base = [inject[t] - dot(conduct[t], volt[t]) for t in range(2)]

    lanes = lax.broadcasted_iota(jnp.int32, (1, 2 * nets), 1)
    tiles = jnp.concatenate([driver_tile[...], driver_tile[...]], axis=1)
    net_of = jnp.where(lanes >= nets, lanes - nets, lanes)
    tile_of = jnp.where(lanes >= nets, 1, 0)
    code = jnp.where(tiles == tile_of, net_of, -1).astype(F32)
    driver_rows = thirds(jnp.concatenate([volt[0, 0:nets, :], volt[1, 0:nets, :]], axis=0))


    pl.semaphore_wait(barrier, len(col_group) + len(row_group) + len(corners))

    def slot_rows(position, count=slots):
        return pl.ds(pl.multiple_of(position * slots, slots), count)

    def exchange(source, target, send, recv, count=slots):
        for peer in col_group:
            pltpu.make_async_remote_copy(
                src_ref=source.at[slot_rows(peer[1], count)],
                dst_ref=target.at[slot_rows(col, count)],
                send_sem=send,
                recv_sem=recv,
                device_id=peer,
                device_id_type=MESH,
            ).start()

    def tile_part(ref, tiles):
        return ref if len(tiles) == 2 else ref.at[tiles[0]]

    def copies(sources, targets, users, send, recv):
        return [
            pltpu.make_async_remote_copy(
                src_ref=tile_part(sources, tiles),
                dst_ref=tile_part(targets.at[i], tiles),
                send_sem=send.at[i],
                recv_sem=recv.at[i],
                device_id=back(offset),
                device_id_type=MESH,
            )
            for i, (offset, tiles) in enumerate(users.items())
        ]

    exchange(ask, asked, ask_send, ask_recv, 1)
    line_copies = [
        pltpu.make_async_remote_copy(
            src_ref=lines,
            dst_ref=lines_in.at[i],
            send_sem=lines_send.at[i],
            recv_sem=lines_recv.at[i],
            device_id=back(offset),
            device_id_type=MESH,
        )
        for i, offset in enumerate(tracks)
    ]
    start_copies = copies(volt.at[:, pl.ds(0, edge)], start_in, sides, start_send, start_recv)
    for copy in line_copies + start_copies:
        copy.start()
    asked[slot_rows(col, 1), :] = ask[slot_rows(col, 1), :]

    r_iota = lax.broadcasted_iota(jnp.int32, (nodes, nodes), 0)
    c_iota = lax.broadcasted_iota(jnp.int32, (nodes, nodes), 1)
    mats = (mat0, mat1)
    for t in range(2):
        mats[t][...] = conduct[t] + jnp.where(r_iota == c_iota, cap[t : t + 1, :], 0.0)
    groups = nodes // 8
    eliminate(mats, 0, groups // 2)

    everything, each = pl.ds(0, (n_col - 1) * slots), pl.ds(0, n_col - 1)
    pltpu.make_async_copy(asked.at[each], asked.at[each], ask_recv).wait()
    wish = asked[pl.ds(0, n_col, stride=slots), :]
    pick = jnp.concatenate(
        [
            jnp.where(jnp.broadcast_to(wish[:, k : k + 1], (n_col, 2 * nets)) == code, 1.0, 0.0)
            for k in range(slots)
        ],
        axis=0,
    ).astype(jnp.bfloat16)
    answer = dot_thirds(pick, driver_rows)
    for k in range(slots):
        give[pl.ds(k, n_col, stride=slots), :] = answer[k * n_col : (k + 1) * n_col]
    exchange(give, given, give_send, give_recv)
    given[slot_rows(col), :] = give[slot_rows(col), :]

    eliminate(mats, groups // 2, groups)
    block_copies = []
    for i, (offset, held) in enumerate(blocks.items()):
        for t in held:
            block_copies.append(
                pltpu.make_async_remote_copy(
                    src_ref=mats[t].at[pl.ds(0, edge)],
                    dst_ref=block_in.at[i, t],
                    send_sem=block_send.at[i, t],
                    recv_sem=block_recv.at[i, t],
                    device_id=back(offset),
                    device_id_type=MESH,
                )
            )
    for copy in block_copies:
        copy.start()

    def inside(offset):
        r, c = offset
        at_row, at_col = row + r, col + c
        return (at_row >= 0) & (at_row < n_row) & (at_col >= 0) & (at_col < n_col)

    present = {o: inside(o) for o in {**wide, **tracks}}

    def home(tile):
        return (tile[0], tile[1] // 2), tile[1] % 2

    def only_inside(tile, value):
        offset = home(tile)[0]
        return value if offset == (0, 0) else jnp.where(present[offset], value, 0.0)

    for copy in line_copies:
        copy.wait_recv()
    eye = lax.broadcasted_iota(jnp.int32, (edge, edge), 0) == lax.broadcasted_iota(
        jnp.int32, (edge, edge), 1
    )
    names = gain_lines(DEPTH - 1)
    place_of = {o: i for i, o in enumerate(tracks)}
    diagonals = []
    for way, tile in names:
        offset, t = home(tile)
        at = 2 * t + way
        if offset == (0, 0):
            line = track[at : at + 1, :]
        else:
            line = lines_in[place_of[offset], at : at + 1, 0:edge]
        diagonals.append(jnp.where(eye, only_inside(tile, line) * SCALE, 0.0))
    columns = dot_thirds(
        thirds(jnp.concatenate(diagonals, axis=0)), jnp.ones((edge, nodes), jnp.bfloat16)
    )
    gains = {name: columns[i * edge : (i + 1) * edge] for i, name in enumerate(names)}

    def flow(tile, field):
        r, c = tile
        v = field[tile]
        total = gains[0, (r, c)] * (v - field[r, c + 1])
        total = total + gains[0, (r, c - 1)] * (v - field[r, c - 1])
        total = total + gains[1, (r, c)] * (v - field[r + 1, c])
        return total + gains[1, (r - 1, c)] * (v - field[r - 1, c])

    def gathered(depth, received, users, mine):
        field = {(0, t): mine[t] for t in range(2)}
        where = {o: i for i, o in enumerate(users)}
        for tile in near(depth):
            offset, t = home(tile)
            if offset != (0, 0):
                field[tile] = only_inside(tile, received[where[offset], t])
        return field

    own_tiles = ((0, 0), (0, 1))
    for copy in start_copies:
        copy.wait_recv()
    start = gathered(1, start_in, sides, [volt[t, 0:edge, :] for t in range(2)])
    first_flow = [flow(tile, start) for tile in own_tiles]
    calm = []
    for t in range(2):
        calm.append(
            jnp.concatenate(
                [base[t][:edge] - first_flow[t] * (1.0 / SCALE), base[t][edge:]], axis=0
            )
        )
    calm_rim = [dot(mats[t][0:edge, :], calm[t]) for t in range(2)]
    spread_rim = jnp.concatenate(
        [dot(mats[t][0:edge, :], scatter[t * nodes : (t + 1) * nodes]) for t in range(2)], axis=0
    )
    pltpu.make_async_copy(given.at[everything], given.at[everything], give_recv).wait()
    lift = dot(spread_rim, given[...])
    own_rim = [calm_rim[t] + lift[t * edge : (t + 1) * edge] for t in range(2)]
    for t in range(2):
        rims[t] = own_rim[t]
    rim_copies = copies(rims, rims_in, wide, rims_send, rims_recv)
    for copy in rim_copies:
        copy.start()
    current = dot(scatter, given[...])
    guess = []
    for t in range(2):
        resid = calm[t] + current[t * nodes : (t + 1) * nodes]
        rest = dot(mats[t][edge:, :], resid)
        guess.append(jnp.concatenate([own_rim[t], rest], axis=0))
        part = column_sum(guess[t], resid)
        moments = [part if t == 0 else moments[0] + part]
    for copy in block_copies:
        copy.wait_recv()
    block = {(0, t): mats[t][0:edge, 0:edge] for t in range(2)}
    block_at = {o: i for i, o in enumerate(blocks)}
    for tile in near(DEPTH - 1):
        offset, t = home(tile)
        if offset != (0, 0):
            block[tile] = block_in[block_at[offset], t, :, 0:edge]
    for copy in rim_copies:
        copy.wait_recv()

    field = gathered(DEPTH, rims_in, wide, own_rim)
    pushed, late_copies = [], []
    for step in range(3):
        reach = DEPTH - 1 - step
        if reach < 0:
            for t in range(2):
                late[t] = field[0, t]
            late_copies = copies(late, late_in, sides, late_send, late_recv)
            for copy in late_copies:
                copy.start()
            for copy in late_copies:
                copy.wait_recv()
            field = gathered(1, late_in, sides, [field[0, t] for t in range(2)])
            reach = 0
        flows = {tile: flow(tile, field) for tile in near(reach)}
        moments.append(sum(column_sum(field[0, t], flows[0, t]) for t in range(2)))
        if step < 2:
            pushed.append([flows[0, t] for t in range(2)])
            field = {
                tile: only_inside(tile, dot(block[tile], flows[tile])) for tile in near(reach)
            }
            moments.append(sum(column_sum(field[0, t], flows[0, t]) for t in range(2)))

    total = jnp.concatenate(moments, axis=0)
    used = pl.ds(0, len(moments))
    for r, (slot, group) in enumerate(((row, row_group), (col, col_group))):
        buf, count = (row_sums, col_sums)[r], len(group) + 1
        buf[slot, used] = total
        for peer in group:
            pltpu.make_async_remote_copy(
                src_ref=buf.at[slot, used],
                dst_ref=buf.at[slot, used],
                send_sem=sum_send.at[r],
                recv_sem=sum_recv.at[r],
                device_id=peer,
                device_id_type=MESH,
            ).start()
        if r == 0:
            lifted = [[dot(mats[t][:, 0:edge], step[t]) for t in range(2)] for step in pushed]
        part = buf.at[pl.ds(0, count - 1), used]
        pltpu.make_async_copy(part, part, sum_recv.at[r]).wait()
        parts = [buf[i, used] for i in range(count)]
        while len(parts) > 1:
            pairs = [parts[i] + parts[i + 1] for i in range(0, len(parts) - 1, 2)]
            parts = pairs + ([parts[-1]] if len(parts) % 2 else [])
        total = parts[0]

    c0, c1, c2 = combination([total[i : i + 1] for i in range(6)])
    for t in range(2):
        out[t] = c0 * guess[t] + c1 * lifted[0][t] + c2 * lifted[1][t]

    for copy in line_copies + start_copies + block_copies + rim_copies + late_copies:
        copy.wait_send()
    pltpu.make_async_copy(ask.at[each], ask.at[each], ask_send).wait()
    pltpu.make_async_copy(give.at[everything], give.at[everything], give_send).wait()
    for r, group in enumerate((row_group, col_group)):
        part = (row_sums, col_sums)[r].at[pl.ds(0, len(group)), used]
        pltpu.make_async_copy(part, part, sum_send.at[r]).wait()


def local(
    initial_voltage,
    inject,
    conduct,
    capacitance,
    track_gain,
    driver_tile,
    sink_net,
    sink_count,
    sink_tile,
    sink_node,
    sink_gain,
):
    n_row, n_col = lax.axis_size("row"), lax.axis_size("col")
    tiles, nodes, patterns = initial_voltage.shape[1:]
    edge = track_gain.shape[-1]
    slots = sink_net.shape[-1]

    def by_slot(array):
        return jnp.swapaxes(array.reshape(n_col, slots), 0, 1)

    block = (tiles, nodes, patterns)
    arrays = (
        initial_voltage.reshape(block),
        inject.reshape(block),
        conduct.reshape(block),
        capacitance.reshape(tiles, nodes),
        track_gain.reshape(2 * tiles, edge),
        driver_tile.reshape(1, -1),
        by_slot(sink_net),
        sink_count.reshape(1, n_col),
        by_slot(sink_tile),
        by_slot(sink_node),
        by_slot(sink_gain),
    )
    rim = (tiles, edge, patterns)
    wide, blocks = from_devices(near(DEPTH)), from_devices(near(DEPTH - 1))
    tracks = from_devices([tile for _, tile in gain_lines(DEPTH - 1)])
    dma = pltpu.SemaphoreType.DMA
    slot_rows = pltpu.VMEM((n_col * slots, patterns), F32)
    result = pl.pallas_call(
        functools.partial(kernel, (n_row, n_col)),
        out_shape=pltpu.VMEM(block, F32),
        in_specs=[pl.BlockSpec(memory_space=pltpu.HBM)] * len(arrays),
        out_specs=pl.BlockSpec(memory_space=pltpu.VMEM),
        scratch_shapes=[
            *[pltpu.VMEM(array.shape, array.dtype) for array in arrays],
            pltpu.VMEM((nodes, nodes), F32),
            pltpu.VMEM((nodes, nodes), F32),
            *[slot_rows] * 4,
            pltpu.VMEM((8, patterns), F32),
            pltpu.VMEM((len(tracks), 8, patterns), F32),
            pltpu.VMEM((4, *rim), F32),
            pltpu.VMEM((len(blocks), *rim), F32),
            pltpu.VMEM(rim, F32),
            pltpu.VMEM((len(wide), *rim), F32),
            pltpu.VMEM(rim, F32),
            pltpu.VMEM((4, *rim), F32),
            pltpu.VMEM((n_row, 8, patterns), F32),
            pltpu.VMEM((n_col, 8, patterns), F32),
            dma((len(arrays),)),
            *[dma] * 4,
            *[dma((len(tracks),))] * 2,
            *[dma((4,))] * 2,
            *[dma((len(blocks), tiles))] * 2,
            *[dma((len(wide),))] * 2,
            *[dma((4,))] * 2,
            *[dma((2,))] * 2,
        ],
        compiler_params=pltpu.CompilerParams(
            collective_id=0, has_side_effects=True
        ),
        name="transient",
    )(*arrays)
    return initial_voltage + result.reshape(initial_voltage.shape)


def solution(mesh):
    four = P("row", "col", None, None)
    three = P("row", "col", None)
    placed = (four, four, four, three, four, three, four, three, four, four, four)
    return jax.shard_map(local, mesh=mesh, in_specs=placed, out_specs=four, check_vma=False)
```
